256 devices in a mesh: slide: 16 (over z_lo, x), band: 16 (over z_hi, y, core).
Axes of the slice: x: 4, y: 4, z: 8 (z_hi: 2, z_lo: 4; z = z_hi * 4 + z_lo), core: 2. Of those that a mesh axis runs over, the one named last changes fastest.
Arguments:
- queries: bfloat16 [131072, 1536], P(('slide', 'band')), parts along dimension 0, may hold values from -200 to 200
- keys: bfloat16 [131072, 1536], P(('slide', 'band')), parts along dimension 0, may hold values from -8 to 8
- values: bfloat16 [131072, 1536], P(('slide', 'band')), parts along dimension 0, may hold values from -6 to 6
- out_gain: float32 [1536], replicated, may hold values from 0.1 to 1.9
- out_weight: bfloat16 [1536, 1536], replicated, may hold values from -0.15625 to 0.15625
- adjacency: int32 [256, 2, 256], P(('slide', 'band')), parts along dimension 0, may hold values from 0 to 511, as said below
- send_counts: int32 [256, 2], P('slide'), parts along dimension 0, may hold values from 1 to 256
- coarse_index: int32 [8192], P(('slide', 'band')), parts along dimension 0, may hold values from 0 to 511, as said below
Outputs:
- context: bfloat16 [131072, 1536], P(('slide', 'band')), parts along dimension 0
The draws below stay inside these ranges and needn't reach their ends.
There are 16 independent parts, one for each index of `slide`. The reference program is written for one: setup_inputs(seed, part) draws one part's arguments, and reference() takes and returns one part's arrays. A program takes and returns all parts, laid end to end along the dimension named above; an argument that names none is the same for every part. Nothing has to cross between parts.
Inputs may be any that keep to these rules, and one draw needn't show every extreme that they name: Within a band, adjacency side 0 lists rows from the first half of the band, side 1 from the second half; entries may repeat; entries at positions from the live count on are padding. `coarse_index`: entry r of a band's block lies in r * 16 to r * 16 + 15.
All inputs are finite; a program needn't handle non-finite values.
Results may differ from the reference program's by a relative error of at most 0.0085.
Values may be sent and summed in bfloat16 or wider, within the bound.
A program may use at most 128 MiB of HBM per device.

```python
import math
import jax
import jax.numpy as jnp
from jax import lax

H = 12
HD = 128
D = 1536
TOK_DEV = 512
DILATION = 16
BMAX = 256
CK = 32
NBANDS = 16
NT = 8192
NC = 512


def shared_pair(key):
    key_draw = jax.random.fold_in(key, 11)
    query_draw = jax.random.fold_in(key, 12)
    key_rows = jnp.clip(jax.random.normal(key_draw, (NT, D), jnp.float32), -6.0, 6.0)
    query_rows = jnp.clip(jax.random.normal(query_draw, (NT, D), jnp.float32), -6.0, 6.0)
    return (query_rows, key_rows)


def draw_queries(key, part):
    return shared_pair(key)[0].astype(jnp.bfloat16)


def draw_keys(key, part):
    return shared_pair(key)[1].astype(jnp.bfloat16)


def boundary_tables(key):
    count_draw = jax.random.fold_in(key, 21)
    pick_draw = jax.random.fold_in(key, 22)
    lower_draw = jax.random.fold_in(key, 23)
    upper_draw = jax.random.fold_in(key, 24)
    counts = jax.random.randint(count_draw, (NBANDS * 2,), 1, BMAX + 1)
    spot = jax.random.randint(pick_draw, (), 0, NBANDS * 2)
    counts = counts.at[spot].set(BMAX).at[(spot + 1) % (NBANDS * 2)].set(1)
    lower = jax.random.randint(lower_draw, (NBANDS, BMAX), 0, TOK_DEV // 2).at[:, 0].set(0)
    upper = jax.random.randint(upper_draw, (NBANDS, BMAX), TOK_DEV // 2, TOK_DEV).at[:, 0].set(TOK_DEV - 1)
    return (jnp.stack([lower, upper], axis=1).astype(jnp.int32), counts.reshape(NBANDS, 2).astype(jnp.int32))


def draw_adjacency(key, part):
    return boundary_tables(key)[0]


def draw_send_counts(key, part):
    return boundary_tables(key)[1]


def draw_coarse_index(key, part):
    offsets = jax.random.randint(jax.random.fold_in(key, 31), (NBANDS, CK), 0, DILATION)
    first_band = jax.random.randint(jax.random.fold_in(key, 32), (), 0, NBANDS)
    last_band = (first_band + 1 + jax.random.randint(jax.random.fold_in(key, 33), (), 0, NBANDS - 1)) % NBANDS
    offsets = offsets.at[first_band, 0].set(0).at[last_band, CK - 1].set(DILATION - 1)
    picked = DILATION * jnp.arange(CK, dtype=jnp.int32)[None, :] + offsets
    return picked.reshape(NC).astype(jnp.int32)


def block_levels(stream_key, dims, shards, least, largest):
    factor_of, own = 1.0, jax.random.fold_in(stream_key, 6)
    for dim, shards_of in shards:
        draws = jnp.exp(jax.random.uniform(jax.random.fold_in(own, dim), (shards_of,), jnp.float32, least / len(shards), largest / len(shards)))
        factor_of = factor_of * jnp.repeat(draws, dims[dim] // shards_of).reshape([-1 if axis == dim else 1 for axis in range(len(dims))])
    return factor_of


def gaussian(stream_key, shape, deviation, bound, shards=(), kind=jnp.bfloat16):
    gain = block_levels(stream_key, shape, shards, -0.22, 0.18) if shards else 1.0
    entries = jax.random.normal(stream_key, shape, jnp.float32) * deviation * gain
    return jnp.minimum(jnp.maximum(entries, -bound), bound).astype(kind)


def setup_inputs(seed: int = 0, part: int = 0) -> dict:
    key_of = jax.random.split(jax.random.key(seed), 9)
    part_splits = jax.random.split(jax.random.fold_in(key_of[8], part), 9)
    return {
        "queries": draw_queries(jax.random.fold_in(jax.random.fold_in(key_of[8], part), 71), part),
        "keys": draw_keys(jax.random.fold_in(jax.random.fold_in(key_of[8], part), 71), part),
        "values": gaussian(part_splits[2], (NT, D), 1.0, 6.0, ((0, 16),)),
        "out_gain": jnp.clip(1.0 + 0.18 * jax.random.normal(key_of[3], (D,), jnp.float32), 0.1, 1.9),
        "out_weight": gaussian(key_of[4], (D, D), D ** -0.5, 0.15625),
        "adjacency": draw_adjacency(jax.random.fold_in(jax.random.fold_in(key_of[8], part), 71), part),
        "send_counts": draw_send_counts(jax.random.fold_in(jax.random.fold_in(key_of[8], part), 71), part),
        "coarse_index": draw_coarse_index(jax.random.fold_in(jax.random.fold_in(key_of[8], part), 71), part),
    }


def reference(queries, keys, values, out_gain, out_weight, adjacency, send_counts, coarse_index):
    coarse_rows = jnp.arange(NC, dtype=jnp.int32) // CK * TOK_DEV + coarse_index.astype(jnp.int32)
    coarse_keys = keys[coarse_rows]
    coarse_values = values[coarse_rows]
    slots = jnp.arange(BMAX, dtype=jnp.int32)
    scale = 1.0 / math.sqrt(HD)

    def one_band(band):
        start = (band * TOK_DEV).astype(jnp.int32)
        query_rows = lax.dynamic_slice_in_dim(queries, start, TOK_DEV, 0)
        local_keys = lax.dynamic_slice_in_dim(keys, start, TOK_DEV, 0)
        local_values = lax.dynamic_slice_in_dim(values, start, TOK_DEV, 0)
        lower = jnp.maximum(band - 1, 0).astype(jnp.int32)
        upper = jnp.minimum(band + 1, NBANDS - 1).astype(jnp.int32)
        lower_rows = lower * TOK_DEV + adjacency[lower, 1]
        upper_rows = upper * TOK_DEV + adjacency[upper, 0]
        lower_live = (slots < send_counts[lower, 1]) & (band > 0)
        upper_live = (slots < send_counts[upper, 0]) & (band < NBANDS - 1)
        all_keys = jnp.concatenate([local_keys, keys[lower_rows], keys[upper_rows], coarse_keys], axis=0)
        all_values = jnp.concatenate([local_values, values[lower_rows], values[upper_rows], coarse_values], axis=0)
        live = jnp.concatenate([jnp.ones((TOK_DEV,), jnp.bool_), lower_live, upper_live, jnp.ones((NC,), jnp.bool_)])
        count = all_keys.shape[0]
        query_heads = query_rows.astype(jnp.float32).reshape(TOK_DEV, H, HD)
        key_heads = all_keys.astype(jnp.float32).reshape(count, H, HD)
        value_heads = all_values.astype(jnp.float32).reshape(count, H, HD)
        scores = jnp.einsum('qhd,khd->hqk', query_heads, key_heads) * scale
        scores = jnp.where(live[None, None, :], scores, -1e+30)
        highest = lax.optimization_barrier(jnp.max(scores, axis=2))
        weights = jnp.exp(scores - highest[:, :, None])
        totals = lax.optimization_barrier(jnp.sum(weights, axis=2))
        rounded = weights.astype(jnp.bfloat16).astype(jnp.float32)
        summed = jnp.einsum('hqk,khd->qhd', rounded, value_heads)
        attended = (summed / jnp.transpose(totals)[:, :, None]).reshape(TOK_DEV, D)
        center = lax.optimization_barrier(jnp.mean(attended, axis=1, keepdims=True))
        shifted = attended - center
        spread = lax.optimization_barrier(jnp.mean(shifted * shifted, axis=1, keepdims=True))
        normed = (shifted / jnp.sqrt(spread + 1e-05) * out_gain.astype(jnp.float32)).astype(jnp.bfloat16)
        return jnp.dot(normed, out_weight, preferred_element_type=jnp.float32).astype(jnp.bfloat16)
    result = lax.map(one_band, jnp.arange(NBANDS, dtype=jnp.int32))
    return result.reshape(NT, D)
```

```python
import jax
import jax.numpy as jnp
from jax import lax
from jax.sharding import PartitionSpec as P

H = 12
HD = 128


BAND = ("zhi", "y", "core")


def shifted_2(block, axis, distance):
    devices = range(16)
    route = [(i - distance, i) for i in devices if i - distance in devices]
    return lax.ppermute(block, axis, route)


def absorb(state, query_heads, key_rows, value_rows, live):
    high_old, total_old, accum_old = state
    count = key_rows.shape[0]
    key_heads = key_rows.reshape(count, H, HD)
    value_heads = value_rows.reshape(count, H, HD)
    scores = jnp.einsum(
        "qhd,khd->hqk", query_heads, key_heads, preferred_element_type=jnp.float32
    ) * (1.0 / HD**0.5)
    scores = jnp.where(live[None, None, :], scores, -1e30)
    high_new = jnp.maximum(high_old, jnp.max(scores, axis=2))
    factor = jnp.exp(high_old - high_new)
    weights = jnp.exp(scores - high_new[:, :, None])
    total_new = total_old * factor + jnp.sum(weights, axis=2)
    summed = jnp.einsum(
        "hqk,khd->qhd",
        weights.astype(jnp.bfloat16),
        value_heads,
        preferred_element_type=jnp.float32,
    )
    accum_new = accum_old * jnp.transpose(factor)[:, :, None] + summed
    return (high_new, total_new, accum_new)


def on_device(queries, keys, values, out_gain, out_weight, adjacency, send_counts, coarse_index):
    rows = queries.shape[0]
    bands = 16
    place = lax.axis_index(BAND)
    width = adjacency.shape[2]
    query_heads = queries.reshape(rows, H, HD)
    lower_rows = adjacency[0, 0]
    upper_rows = adjacency[0, 1]
    to_lower = jnp.stack([keys[lower_rows], values[lower_rows]], axis=1)
    to_upper = jnp.stack([keys[upper_rows], values[upper_rows]], axis=1)
    coarse = jnp.stack([keys[coarse_index], values[coarse_index]], axis=1)
    from_lower = shifted_2(to_upper, BAND, 1)
    from_upper = shifted_2(to_lower, BAND, -1)
    state = (
        jnp.full((H, rows), -1e30, jnp.float32),
        jnp.zeros((H, rows), jnp.float32),
        jnp.zeros((rows, H, HD), jnp.float32),
    )
    state = absorb(state, query_heads, keys, values, jnp.ones((rows,), jnp.bool_))
    lower_peer = jnp.maximum(place - 1, 0)
    upper_peer = jnp.minimum(place + 1, bands - 1)
    slots = jnp.arange(width, dtype=jnp.int32)
    lower_live = (slots < send_counts[lower_peer, 1]) & (place > 0)
    upper_live = (slots < send_counts[upper_peer, 0]) & (place < bands - 1)
    state = absorb(state, query_heads, from_lower[:, 0], from_lower[:, 1], lower_live)
    state = absorb(state, query_heads, from_upper[:, 0], from_upper[:, 1], upper_live)
    halves = lax.all_gather(coarse, "zhi", axis=0, tiled=True)
    everything = lax.all_gather(halves, ("y", "core"), axis=0, tiled=True)
    state = absorb(
        state,
        query_heads,
        everything[:, 0],
        everything[:, 1],
        jnp.ones((everything.shape[0],), jnp.bool_),
    )
    totals = state[1]
    accum = state[2]
    attended = (accum / jnp.transpose(totals)[:, :, None]).reshape(rows, H * HD)
    center = jnp.mean(attended, axis=1, keepdims=True)
    shifted = attended - center
    spread = jnp.mean(shifted * shifted, axis=1, keepdims=True)
    normed = (shifted / jnp.sqrt(spread + 1e-05) * out_gain).astype(jnp.bfloat16)
    return jnp.dot(normed, out_weight, preferred_element_type=jnp.float32).astype(jnp.bfloat16)


def solution(mesh):
    grid = mesh.devices.reshape(mesh.devices.shape[0], 2, 4, 2)
    fine = jax.sharding.Mesh(grid, ("slide",) + BAND)
    rows = ("slide",) + BAND
    in_specs = (
        P(rows, None),
        P(rows, None),
        P(rows, None),
        P(),
        P(),
        P(rows, None, None),
        P("slide", None),
        P(rows),
    )
    out_specs = P(rows, None)
    return jax.shard_map(
        on_device, mesh=fine, in_specs=in_specs, out_specs=out_specs, check_vma=False
    )
```

```python
import functools
import jax
import jax.numpy as jnp
from jax import lax
from jax.experimental import pallas as pl
from jax.experimental.pallas import tpu as pltpu
from jax.sharding import PartitionSpec as P

H = 12
HD = 128
BAND = ("zhi", "y", "core")
TQ = 128


def shifted_2(block, axis, distance):
    devices = range(16)
    route = [(i - distance, i) for i in devices if i - distance in devices]
    return lax.ppermute(block, axis, route)


def attend_kernel(q_ref, k_ref, v_ref, lo_ref, up_ref, co_ref, mlo_ref, mup_ref,
                  gain_ref, w_ref, o_ref, s_ref, att_ref):
    n_loc = k_ref.shape[0]
    n_b = lo_ref.shape[1]
    n_c = co_ref.shape[1]
    segs = [
        (k_ref, v_ref, 0, None),
        (lo_ref.at[0], lo_ref.at[1], n_loc, mlo_ref),
        (up_ref.at[0], up_ref.at[1], n_loc + n_b, mup_ref),
        (co_ref.at[0], co_ref.at[1], n_loc + 2 * n_b, None),
    ]
    scale = 1.0 / HD**0.5
    for h in range(H):
        cols = slice(h * HD, (h + 1) * HD)
        qh = q_ref[:, cols]
        for kr, _, off, mr in segs:
            n = kr.shape[0]
            s = lax.dot_general(
                qh, kr[:, cols], (((1,), (1,)), ((), ())),
                preferred_element_type=jnp.float32,
            ) * scale
            if mr is not None:
                s = jnp.where(mr[...] > 0.5, s, -1e30)
            s_ref[:, off:off + n] = s
        sc = s_ref[...]
        high = jnp.max(sc, axis=1, keepdims=True)
        w = jnp.exp(sc - high)
        total = jnp.sum(w, axis=1, keepdims=True)
        wb = w.astype(jnp.bfloat16)
        acc = None
        for kr, vr, off, _ in segs:
            n = kr.shape[0]
            part = jnp.dot(wb[:, off:off + n], vr[:, cols],
                           preferred_element_type=jnp.float32)
            acc = part if acc is None else acc + part
        att_ref[:, cols] = acc / total
    att = att_ref[...]
    center = jnp.mean(att, axis=1, keepdims=True)
    shifted = att - center
    spread = jnp.mean(shifted * shifted, axis=1, keepdims=True)
    normed = (shifted / jnp.sqrt(spread + 1e-05) * gain_ref[...]).astype(jnp.bfloat16)
    o_ref[...] = jnp.dot(normed, w_ref[...],
                         preferred_element_type=jnp.float32).astype(o_ref.dtype)


def attend(queries, keys, values, lo, up, co, mlo, mup, gain, weight):
    rows, width = queries.shape
    nk = keys.shape[0] + 2 * lo.shape[1] + co.shape[1]
    full2 = lambda a: pl.BlockSpec(a.shape, lambda i: (0,) * a.ndim)
    return pl.pallas_call(
        attend_kernel,
        out_shape=jax.ShapeDtypeStruct((rows, width), jnp.bfloat16),
        grid=(rows // TQ,),
        in_specs=[
            pl.BlockSpec((TQ, width), lambda i: (i, 0)),
            full2(keys), full2(values), full2(lo), full2(up), full2(co),
            full2(mlo), full2(mup), full2(gain), full2(weight),
        ],
        out_specs=pl.BlockSpec((TQ, width), lambda i: (i, 0)),
        scratch_shapes=[
            pltpu.VMEM((TQ, nk), jnp.float32),
            pltpu.VMEM((TQ, width), jnp.float32),
        ],
        compiler_params=pltpu.CompilerParams(vmem_limit_bytes=60 * 1024 * 1024),
    )(queries, keys, values, lo, up, co, mlo, mup, gain, weight)


def on_device(queries, keys, values, out_gain, out_weight, adjacency, send_counts, coarse_index):
    bands = 16
    place = lax.axis_index(BAND)
    width = adjacency.shape[2]
    lower_rows = adjacency[0, 0]
    upper_rows = adjacency[0, 1]
    to_lower = jnp.stack([keys[lower_rows], values[lower_rows]], axis=0)
    to_upper = jnp.stack([keys[upper_rows], values[upper_rows]], axis=0)
    coarse = jnp.stack([keys[coarse_index], values[coarse_index]], axis=0)
    from_lower = shifted_2(to_upper, BAND, 1)
    from_upper = shifted_2(to_lower, BAND, -1)
    halves = lax.all_gather(coarse, "zhi", axis=1, tiled=True)
    everything = lax.all_gather(halves, ("y", "core"), axis=1, tiled=True)
    lower_peer = jnp.maximum(place - 1, 0)
    upper_peer = jnp.minimum(place + 1, bands - 1)
    slots = jnp.arange(width, dtype=jnp.int32)
    lower_live = (slots < send_counts[lower_peer, 1]) & (place > 0)
    upper_live = (slots < send_counts[upper_peer, 0]) & (place < bands - 1)
    mlo = lower_live.astype(jnp.float32)[None, :]
    mup = upper_live.astype(jnp.float32)[None, :]
    return attend(queries, keys, values, from_lower, from_upper, everything,
                  mlo, mup, out_gain[None, :], out_weight)


def solution(mesh):
    grid = mesh.devices.reshape(mesh.devices.shape[0], 2, 4, 2)
    fine = jax.sharding.Mesh(grid, ("slide",) + BAND)
    rows = ("slide",) + BAND
    in_specs = (
        P(rows, None),
        P(rows, None),
        P(rows, None),
        P(),
        P(),
        P(rows, None, None),
        P("slide", None),
        P(rows),
    )
    out_specs = P(rows, None)
    return jax.shard_map(
        on_device, mesh=fine, in_specs=in_specs, out_specs=out_specs, check_vma=False
    )
```

```python
import functools
import jax
import jax.numpy as jnp
from jax import lax
from jax.experimental import pallas as pl
from jax.experimental.pallas import tpu as pltpu
from jax.sharding import PartitionSpec as P

H = 12
HD = 128
BAND = ("zhi", "y", "core")
TQ = 128


def shifted_2(block, axis, distance):
    devices = range(16)
    route = [(i - distance, i) for i in devices if i - distance in devices]
    return lax.ppermute(block, axis, route)


def attend_kernel(q_ref, k_ref, v_ref, lo_ref, up_ref, co_ref, mlo_ref, mup_ref,
                  gain_ref, w_ref, o_ref, s_ref, att_ref):
    n_loc = k_ref.shape[0]
    n_b = lo_ref.shape[1]
    n_c = co_ref.shape[1]
    segs = [
        (k_ref, v_ref, 0, None),
        (lo_ref.at[0], lo_ref.at[1], n_loc, mlo_ref),
        (up_ref.at[0], up_ref.at[1], n_loc + n_b, mup_ref),
        (co_ref.at[0], co_ref.at[1], n_loc + 2 * n_b, None),
    ]
    scale = 1.0 / HD**0.5
    for h in range(H):
        cols = slice(h * HD, (h + 1) * HD)
        qh = q_ref[:, cols]
        for kr, _, off, mr in segs:
            n = kr.shape[0]
            s = lax.dot_general(
                qh, kr[:, cols], (((1,), (1,)), ((), ())),
                preferred_element_type=jnp.float32,
            ) * scale
            if mr is not None:
                s = jnp.where(mr[...] > 0.5, s, -1e30)
            s_ref[:, off:off + n] = s
        sc = s_ref[...]
        high = jnp.max(sc, axis=1, keepdims=True)
        w = jnp.exp(sc - high)
        total = jnp.sum(w, axis=1, keepdims=True)
        wb = w.astype(jnp.bfloat16)
        acc = None
        for kr, vr, off, _ in segs:
            n = kr.shape[0]
            part = jnp.dot(wb[:, off:off + n], vr[:, cols],
                           preferred_element_type=jnp.float32)
            acc = part if acc is None else acc + part
        att_ref[:, cols] = acc / total
    att = att_ref[...]
    center = jnp.mean(att, axis=1, keepdims=True)
    shifted = att - center
    spread = jnp.mean(shifted * shifted, axis=1, keepdims=True)
    normed = (shifted / jnp.sqrt(spread + 1e-05) * gain_ref[...]).astype(jnp.bfloat16)
    o_ref[...] = jnp.dot(normed, w_ref[...],
                         preferred_element_type=jnp.float32).astype(o_ref.dtype)


def attend(queries, keys, values, lo, up, co, mlo, mup, gain, weight):
    rows, width = queries.shape
    nk = keys.shape[0] + 2 * lo.shape[1] + co.shape[1]
    full2 = lambda a: pl.BlockSpec(a.shape, lambda i: (0,) * a.ndim)
    return pl.pallas_call(
        attend_kernel,
        out_shape=jax.ShapeDtypeStruct((rows, width), jnp.bfloat16),
        grid=(rows // TQ,),
        in_specs=[
            pl.BlockSpec((TQ, width), lambda i: (i, 0)),
            full2(keys), full2(values), full2(lo), full2(up), full2(co),
            full2(mlo), full2(mup), full2(gain), full2(weight),
        ],
        out_specs=pl.BlockSpec((TQ, width), lambda i: (i, 0)),
        scratch_shapes=[
            pltpu.VMEM((TQ, nk), jnp.float32),
            pltpu.VMEM((TQ, width), jnp.float32),
        ],
        compiler_params=pltpu.CompilerParams(vmem_limit_bytes=60 * 1024 * 1024),
    )(queries, keys, values, lo, up, co, mlo, mup, gain, weight)


def on_device(queries, keys, values, out_gain, out_weight, adjacency, send_counts, coarse_index):
    bands = 16
    place = lax.axis_index(BAND)
    width = adjacency.shape[2]
    lower_rows = adjacency[0, 0]
    upper_rows = adjacency[0, 1]
    to_lower = jnp.stack([keys[lower_rows], values[lower_rows]], axis=0)
    to_upper = jnp.stack([keys[upper_rows], values[upper_rows]], axis=0)
    coarse = jnp.stack([keys[coarse_index], values[coarse_index]], axis=0)
    from_lower = shifted_2(to_upper, BAND, 1)
    from_upper = shifted_2(to_lower, BAND, -1)
    partner = lax.ppermute(coarse, "zhi", [(0, 1), (1, 0)])
    halves = jnp.concatenate([coarse, partner], axis=1)
    chips = lax.all_gather(halves, "y", axis=1, tiled=True)
    everything = lax.all_gather(chips, "core", axis=1, tiled=True)
    lower_peer = jnp.maximum(place - 1, 0)
    upper_peer = jnp.minimum(place + 1, bands - 1)
    slots = jnp.arange(width, dtype=jnp.int32)
    lower_live = (slots < send_counts[lower_peer, 1]) & (place > 0)
    upper_live = (slots < send_counts[upper_peer, 0]) & (place < bands - 1)
    mlo = lower_live.astype(jnp.float32)[None, :]
    mup = upper_live.astype(jnp.float32)[None, :]
    return attend(queries, keys, values, from_lower, from_upper, everything,
                  mlo, mup, out_gain[None, :], out_weight)


def solution(mesh):
    grid = mesh.devices.reshape(mesh.devices.shape[0], 2, 4, 2)
    fine = jax.sharding.Mesh(grid, ("slide",) + BAND)
    rows = ("slide",) + BAND
    in_specs = (
        P(rows, None),
        P(rows, None),
        P(rows, None),
        P(),
        P(),
        P(rows, None, None),
        P("slide", None),
        P(rows),
    )
    out_specs = P(rows, None)
    return jax.shard_map(
        on_device, mesh=fine, in_specs=in_specs, out_specs=out_specs, check_vma=False
    )
```

```python
import functools
import jax
import jax.numpy as jnp
from jax import lax
from jax.experimental import pallas as pl
from jax.experimental.pallas import tpu as pltpu
from jax.sharding import PartitionSpec as P

H = 12
HD = 128
BAND = ("zhi", "y", "core")
TQ = 128


def shifted_2(block, axis, distance):
    devices = range(16)
    route = [(i - distance, i) for i in devices if i - distance in devices]
    return lax.ppermute(block, axis, route)


def attend_kernel(q_ref, k_ref, v_ref, lo_ref, up_ref, co_ref, mlo_ref, mup_ref,
                  gain_ref, w_ref, o_ref, s_ref, att_ref):
    n_loc = k_ref.shape[0]
    n_b = lo_ref.shape[1]
    n_c = co_ref.shape[1]
    segs = [
        (k_ref, v_ref, 0, None),
        (lo_ref.at[0], lo_ref.at[1], n_loc, mlo_ref),
        (up_ref.at[0], up_ref.at[1], n_loc + n_b, mup_ref),
        (co_ref.at[0], co_ref.at[1], n_loc + 2 * n_b, None),
    ]
    scale = 1.0 / HD**0.5
    for h in range(H):
        cols = slice(h * HD, (h + 1) * HD)
        qh = q_ref[:, cols]
        for kr, _, off, mr in segs:
            n = kr.shape[0]
            s = lax.dot_general(
                qh, kr[:, cols], (((1,), (1,)), ((), ())),
                preferred_element_type=jnp.float32,
            ) * scale
            if mr is not None:
                s = jnp.where(mr[...] > 0.5, s, -1e30)
            s_ref[:, off:off + n] = s
        sc = s_ref[...]
        high = jnp.max(sc, axis=1, keepdims=True)
        w = jnp.exp(sc - high)
        total = jnp.sum(w, axis=1, keepdims=True)
        wb = w.astype(jnp.bfloat16)
        acc = None
        for kr, vr, off, _ in segs:
            n = kr.shape[0]
            part = jnp.dot(wb[:, off:off + n], vr[:, cols],
                           preferred_element_type=jnp.float32)
            acc = part if acc is None else acc + part
        att_ref[:, cols] = acc / total
    att = att_ref[...]
    center = jnp.mean(att, axis=1, keepdims=True)
    shifted = att - center
    spread = jnp.mean(shifted * shifted, axis=1, keepdims=True)
    normed = (shifted / jnp.sqrt(spread + 1e-05) * gain_ref[...]).astype(jnp.bfloat16)
    o_ref[...] = jnp.dot(normed, w_ref[...],
                         preferred_element_type=jnp.float32).astype(o_ref.dtype)


def attend(queries, keys, values, lo, up, co, mlo, mup, gain, weight):
    rows, width = queries.shape
    nk = keys.shape[0] + 2 * lo.shape[1] + co.shape[1]
    full2 = lambda a: pl.BlockSpec(a.shape, lambda i: (0,) * a.ndim)
    return pl.pallas_call(
        attend_kernel,
        out_shape=jax.ShapeDtypeStruct((rows, width), jnp.bfloat16),
        grid=(rows // TQ,),
        in_specs=[
            pl.BlockSpec((TQ, width), lambda i: (i, 0)),
            full2(keys), full2(values), full2(lo), full2(up), full2(co),
            full2(mlo), full2(mup), full2(gain), full2(weight),
        ],
        out_specs=pl.BlockSpec((TQ, width), lambda i: (i, 0)),
        scratch_shapes=[
            pltpu.VMEM((TQ, nk), jnp.float32),
            pltpu.VMEM((TQ, width), jnp.float32),
        ],
        compiler_params=pltpu.CompilerParams(vmem_limit_bytes=60 * 1024 * 1024),
    )(queries, keys, values, lo, up, co, mlo, mup, gain, weight)


def exchange_kernel(co_ref, tl_ref, tu_ref, co_all, lo_in, up_in,
                    send_a, send_b, send_bd, recv_co, recv_bd, local_sem):
    slide = lax.axis_index("slide")
    zh = lax.axis_index("zhi")
    yy = lax.axis_index("y")
    cc = lax.axis_index("core")
    here = yy * 2 + cc
    band = zh * 8 + here
    pband = (1 - zh) * 8 + here

    def dev(z, spot):
        return (slide, z, spot // 2, spot % 2)

    def coarse_copy(src, slot, sem, target):
        return pltpu.make_async_remote_copy(
            src_ref=src, dst_ref=co_all.at[:, slot], send_sem=sem,
            recv_sem=recv_co.at[slot], device_id=target,
            device_id_type=pl.DeviceIdType.MESH)

    own = pltpu.make_async_copy(co_ref, co_all.at[:, band], local_sem.at[0])
    own.start()
    first = []
    for d in range(1, 8):
        spot = (here + d) % 8
        c = coarse_copy(co_ref, band, send_a.at[d - 1], dev(zh, spot))
        c.start()
        first.append(c)
    across = coarse_copy(co_ref, band, send_a.at[7], dev(1 - zh, here))
    across.start()

    up_band = band + 1
    low_band = band - 1
    to_up = pltpu.make_async_remote_copy(
        src_ref=tu_ref, dst_ref=lo_in, send_sem=send_bd.at[0], recv_sem=recv_bd.at[0],
        device_id=dev(up_band // 8, up_band % 8), device_id_type=pl.DeviceIdType.MESH)
    to_low = pltpu.make_async_remote_copy(
        src_ref=tl_ref, dst_ref=up_in, send_sem=send_bd.at[1], recv_sem=recv_bd.at[1],
        device_id=dev(low_band // 8, low_band % 8), device_id_type=pl.DeviceIdType.MESH)
    fill_lo = pltpu.make_async_copy(tl_ref, lo_in, local_sem.at[1])
    fill_up = pltpu.make_async_copy(tu_ref, up_in, local_sem.at[2])

    @pl.when(band < 15)
    def _():
        to_up.start()

    @pl.when(band > 0)
    def _():
        to_low.start()

    @pl.when(band == 0)
    def _():
        fill_lo.start()

    @pl.when(band == 15)
    def _():
        fill_up.start()

    coarse_copy(co_ref, pband, send_a.at[0], dev(1 - zh, here)).wait_recv()
    relay = []
    for d in range(1, 8):
        spot = (here + d) % 8
        c = coarse_copy(co_all.at[:, pband], pband, send_b.at[d - 1], dev(zh, spot))
        c.start()
        relay.append(c)

    own.wait()
    for c in first:
        c.wait_send()
    across.wait_send()
    for c in relay:
        c.wait_send()
    for d in range(1, 8):
        spot = (here + d) % 8
        coarse_copy(co_ref, zh * 8 + spot, send_a.at[0], dev(zh, spot)).wait_recv()
        coarse_copy(co_ref, (1 - zh) * 8 + spot, send_a.at[0], dev(zh, spot)).wait_recv()

    @pl.when(band < 15)
    def _():
        to_up.wait_send()
        to_low.wait_recv()

    @pl.when(band > 0)
    def _():
        to_low.wait_send()
        to_up.wait_recv()

    @pl.when(band == 0)
    def _():
        fill_lo.wait()

    @pl.when(band == 15)
    def _():
        fill_up.wait()


def exchange(coarse, to_lower, to_upper):
    two, ck, width = coarse.shape
    nb = to_lower.shape[1]
    anyspec = pl.BlockSpec(memory_space=pl.ANY)
    return pl.pallas_call(
        exchange_kernel,
        out_shape=(
            jax.ShapeDtypeStruct((two, 16, ck, width), coarse.dtype),
            jax.ShapeDtypeStruct((two, nb, width), coarse.dtype),
            jax.ShapeDtypeStruct((two, nb, width), coarse.dtype),
        ),
        in_specs=[anyspec] * 3,
        out_specs=(anyspec,) * 3,
        scratch_shapes=[
            pltpu.SemaphoreType.DMA((8,)),
            pltpu.SemaphoreType.DMA((7,)),
            pltpu.SemaphoreType.DMA((2,)),
            pltpu.SemaphoreType.DMA((16,)),
            pltpu.SemaphoreType.DMA((2,)),
            pltpu.SemaphoreType.DMA((3,)),
        ],
        compiler_params=pltpu.CompilerParams(has_side_effects=True),
    )(coarse, to_lower, to_upper)


def on_device(queries, keys, values, out_gain, out_weight, adjacency, send_counts, coarse_index):
    bands = 16
    place = lax.axis_index(BAND)
    width = adjacency.shape[2]
    lower_rows = adjacency[0, 0]
    upper_rows = adjacency[0, 1]
    to_lower = jnp.stack([keys[lower_rows], values[lower_rows]], axis=0)
    to_upper = jnp.stack([keys[upper_rows], values[upper_rows]], axis=0)
    coarse = jnp.stack([keys[coarse_index], values[coarse_index]], axis=0)
    gathered, from_lower, from_upper = exchange(coarse, to_lower, to_upper)
    everything = gathered.reshape(2, -1, gathered.shape[-1])
    lower_peer = jnp.maximum(place - 1, 0)
    upper_peer = jnp.minimum(place + 1, bands - 1)
    slots = jnp.arange(width, dtype=jnp.int32)
    lower_live = (slots < send_counts[lower_peer, 1]) & (place > 0)
    upper_live = (slots < send_counts[upper_peer, 0]) & (place < bands - 1)
    mlo = lower_live.astype(jnp.float32)[None, :]
    mup = upper_live.astype(jnp.float32)[None, :]
    return attend(queries, keys, values, from_lower, from_upper, everything,
                  mlo, mup, out_gain[None, :], out_weight)


def solution(mesh):
    grid = mesh.devices.reshape(mesh.devices.shape[0], 2, 4, 2)
    fine = jax.sharding.Mesh(grid, ("slide",) + BAND)
    rows = ("slide",) + BAND
    in_specs = (
        P(rows, None),
        P(rows, None),
        P(rows, None),
        P(),
        P(),
        P(rows, None, None),
        P("slide", None),
        P(rows),
    )
    out_specs = P(rows, None)
    return jax.shard_map(
        on_device, mesh=fine, in_specs=in_specs, out_specs=out_specs, check_vma=False
    )
```

```python
import functools
import jax
import jax.numpy as jnp
from jax import lax
from jax.experimental import pallas as pl
from jax.experimental.pallas import tpu as pltpu
from jax.sharding import PartitionSpec as P

H = 12
HD = 128
BAND = ("zhi", "y", "core")
TQ = 128


def shifted_2(block, axis, distance):
    devices = range(16)
    route = [(i - distance, i) for i in devices if i - distance in devices]
    return lax.ppermute(block, axis, route)


def first_kernel(q_ref, k_ref, v_ref, lo_ref, up_ref, mlo_ref, mup_ref,
                 acc_ref, m_ref, l_ref, s_ref):
    n_loc = k_ref.shape[0]
    n_b = lo_ref.shape[1]
    segs = [
        (k_ref, v_ref, 0, None),
        (lo_ref.at[0], lo_ref.at[1], n_loc, mlo_ref),
        (up_ref.at[0], up_ref.at[1], n_loc + n_b, mup_ref),
    ]
    scale = 1.0 / HD**0.5
    for h in range(H):
        cols = slice(h * HD, (h + 1) * HD)
        qh = q_ref[:, cols]
        for kr, _, off, mr in segs:
            n = kr.shape[0]
            s = lax.dot_general(
                qh, kr[:, cols], (((1,), (1,)), ((), ())),
                preferred_element_type=jnp.float32,
            ) * scale
            if mr is not None:
                s = jnp.where(mr[...] > 0.5, s, -1e30)
            s_ref[:, off:off + n] = s
        sc = s_ref[...]
        high = jnp.max(sc, axis=1, keepdims=True)
        w = jnp.exp(sc - high)
        total = jnp.sum(w, axis=1, keepdims=True)
        wb = w.astype(jnp.bfloat16)
        acc = None
        for kr, vr, off, _ in segs:
            n = kr.shape[0]
            part = jnp.dot(wb[:, off:off + n], vr[:, cols],
                           preferred_element_type=jnp.float32)
            acc = part if acc is None else acc + part
        acc_ref[:, cols] = acc
        m_ref[:, h:h + 1] = high
        l_ref[:, h:h + 1] = total


def last_kernel(q_ref, co_ref, acc_ref, m_ref, l_ref, gain_ref, w_ref, o_ref, att_ref):
    scale = 1.0 / HD**0.5
    kr = co_ref.at[0]
    vr = co_ref.at[1]
    for h in range(H):
        cols = slice(h * HD, (h + 1) * HD)
        s = lax.dot_general(
            q_ref[:, cols], kr[:, cols], (((1,), (1,)), ((), ())),
            preferred_element_type=jnp.float32,
        ) * scale
        high_old = m_ref[:, h:h + 1]
        high = jnp.maximum(high_old, jnp.max(s, axis=1, keepdims=True))
        factor = jnp.exp(high_old - high)
        w = jnp.exp(s - high)
        total = l_ref[:, h:h + 1] * factor + jnp.sum(w, axis=1, keepdims=True)
        acc = acc_ref[:, cols] * factor + jnp.dot(
            w.astype(jnp.bfloat16), vr[:, cols], preferred_element_type=jnp.float32)
        att_ref[:, cols] = acc / total
    att = att_ref[...]
    center = jnp.mean(att, axis=1, keepdims=True)
    shifted = att - center
    spread = jnp.mean(shifted * shifted, axis=1, keepdims=True)
    normed = (shifted / jnp.sqrt(spread + 1e-05) * gain_ref[...]).astype(jnp.bfloat16)
    o_ref[...] = jnp.dot(normed, w_ref[...],
                         preferred_element_type=jnp.float32).astype(o_ref.dtype)


def whole(a):
    return pl.BlockSpec(a.shape, lambda i: (0,) * a.ndim)


def attend_first(queries, keys, values, lo, up, mlo, mup):
    rows, width = queries.shape
    nk = keys.shape[0] + 2 * lo.shape[1]
    rowblock = pl.BlockSpec((TQ, width), lambda i: (i, 0))
    lane = pl.BlockSpec((TQ, 128), lambda i: (i, 0))
    return pl.pallas_call(
        first_kernel,
        out_shape=(
            jax.ShapeDtypeStruct((rows, width), jnp.float32),
            jax.ShapeDtypeStruct((rows, 128), jnp.float32),
            jax.ShapeDtypeStruct((rows, 128), jnp.float32),
        ),
        grid=(rows // TQ,),
        in_specs=[rowblock, whole(keys), whole(values), whole(lo), whole(up),
                  whole(mlo), whole(mup)],
        out_specs=(rowblock, lane, lane),
        scratch_shapes=[pltpu.VMEM((TQ, nk), jnp.float32)],
        compiler_params=pltpu.CompilerParams(vmem_limit_bytes=60 * 1024 * 1024),
        cost_estimate=pl.CostEstimate(
            flops=4 * rows * nk * width, transcendentals=rows * nk * H,
            bytes_accessed=2 * width * (rows + 2 * nk) + 4 * rows * width),
    )(queries, keys, values, lo, up, mlo, mup)


def attend_last(queries, co, acc, high, total, gain, weight):
    rows, width = queries.shape
    rowblock = pl.BlockSpec((TQ, width), lambda i: (i, 0))
    lane = pl.BlockSpec((TQ, 128), lambda i: (i, 0))
    return pl.pallas_call(
        last_kernel,
        out_shape=jax.ShapeDtypeStruct((rows, width), jnp.bfloat16),
        grid=(rows // TQ,),
        in_specs=[rowblock, whole(co), rowblock, lane, lane, whole(gain), whole(weight)],
        out_specs=rowblock,
        scratch_shapes=[pltpu.VMEM((TQ, width), jnp.float32)],
        compiler_params=pltpu.CompilerParams(vmem_limit_bytes=60 * 1024 * 1024),
    )(queries, co, acc, high, total, gain, weight)


def on_device(queries, keys, values, out_gain, out_weight, adjacency, send_counts, coarse_index):
    bands = 16
    place = lax.axis_index(BAND)
    width = adjacency.shape[2]
    lower_rows = adjacency[0, 0]
    upper_rows = adjacency[0, 1]
    to_lower = jnp.stack([keys[lower_rows], values[lower_rows]], axis=0)
    to_upper = jnp.stack([keys[upper_rows], values[upper_rows]], axis=0)
    coarse = jnp.stack([keys[coarse_index], values[coarse_index]], axis=0)
    from_lower = shifted_2(to_upper, BAND, 1)
    from_upper = shifted_2(to_lower, BAND, -1)
    halves = lax.all_gather(coarse, "zhi", axis=1, tiled=True)
    everything = lax.all_gather(halves, ("y", "core"), axis=1, tiled=True)
    lower_peer = jnp.maximum(place - 1, 0)
    upper_peer = jnp.minimum(place + 1, bands - 1)
    slots = jnp.arange(width, dtype=jnp.int32)
    lower_live = (slots < send_counts[lower_peer, 1]) & (place > 0)
    upper_live = (slots < send_counts[upper_peer, 0]) & (place < bands - 1)
    mlo = lower_live.astype(jnp.float32)[None, :]
    mup = upper_live.astype(jnp.float32)[None, :]
    acc, high, total = attend_first(queries, keys, values, from_lower, from_upper, mlo, mup)
    return attend_last(queries, everything, acc, high, total, out_gain[None, :], out_weight)


def solution(mesh):
    grid = mesh.devices.reshape(mesh.devices.shape[0], 2, 4, 2)
    fine = jax.sharding.Mesh(grid, ("slide",) + BAND)
    rows = ("slide",) + BAND
    in_specs = (
        P(rows, None),
        P(rows, None),
        P(rows, None),
        P(),
        P(),
        P(rows, None, None),
        P("slide", None),
        P(rows),
    )
    out_specs = P(rows, None)
    return jax.shard_map(
        on_device, mesh=fine, in_specs=in_specs, out_specs=out_specs, check_vma=False
    )
```

```python
import functools
import jax
import jax.numpy as jnp
from jax import lax
from jax.experimental import pallas as pl
from jax.experimental.pallas import tpu as pltpu
from jax.sharding import PartitionSpec as P

H = 12
HD = 128
BAND = ("zhi", "y", "core")
TQ = 128


def shifted_2(block, axis, distance):
    devices = range(16)
    route = [(i - distance, i) for i in devices if i - distance in devices]
    return lax.ppermute(block, axis, route)


def scores(qh, kr, cols, mr):
    s = lax.dot_general(
        qh, kr[:, cols], (((1,), (1,)), ((), ())),
        preferred_element_type=jnp.float32,
    ) * (1.0 / HD**0.5)
    if mr is not None:
        s = jnp.where(mr[...] > 0.5, s, -1e30)
    return s


def first_kernel(q_ref, k_ref, v_ref, acc_ref, m_ref, l_ref):
    for h in range(H):
        cols = slice(h * HD, (h + 1) * HD)
        sc = scores(q_ref[:, cols], k_ref, cols, None)
        high = jnp.max(sc, axis=1, keepdims=True)
        w = jnp.exp(sc - high)
        acc_ref[:, cols] = jnp.dot(w.astype(jnp.bfloat16), v_ref[:, cols],
                                   preferred_element_type=jnp.float32)
        m_ref[:, h:h + 1] = high
        l_ref[:, h:h + 1] = jnp.sum(w, axis=1, keepdims=True)


def last_kernel(q_ref, lo_ref, up_ref, co_ref, mlo_ref, mup_ref, acc_ref, m_ref, l_ref,
                gain_ref, o_ref, s_ref, att_ref):
    n_b = lo_ref.shape[1]
    segs = [
        (lo_ref.at[0], lo_ref.at[1], 0, mlo_ref),
        (up_ref.at[0], up_ref.at[1], n_b, mup_ref),
        (co_ref.at[0], co_ref.at[1], 2 * n_b, None),
    ]
    for h in range(H):
        cols = slice(h * HD, (h + 1) * HD)
        qh = q_ref[:, cols]
        for kr, _, off, mr in segs:
            s_ref[:, off:off + kr.shape[0]] = scores(qh, kr, cols, mr)
        sc = s_ref[...]
        high_old = m_ref[:, h:h + 1]
        high = jnp.maximum(high_old, jnp.max(sc, axis=1, keepdims=True))
        factor = jnp.exp(high_old - high)
        w = jnp.exp(sc - high)
        total = l_ref[:, h:h + 1] * factor + jnp.sum(w, axis=1, keepdims=True)
        wb = w.astype(jnp.bfloat16)
        acc = acc_ref[:, cols] * factor
        for kr, vr, off, _ in segs:
            n = kr.shape[0]
            acc = acc + jnp.dot(wb[:, off:off + n], vr[:, cols],
                                preferred_element_type=jnp.float32)
        att_ref[:, cols] = acc / total
    att = att_ref[...]
    center = jnp.mean(att, axis=1, keepdims=True)
    shifted = att - center
    spread = jnp.mean(shifted * shifted, axis=1, keepdims=True)
    o_ref[...] = (shifted / jnp.sqrt(spread + 1e-05) * gain_ref[...]).astype(o_ref.dtype)


def whole(a):
    return pl.BlockSpec(a.shape, lambda i: (0,) * a.ndim)


def attend_first(queries, keys, values):
    rows, width = queries.shape
    nk = keys.shape[0]
    rowblock = pl.BlockSpec((TQ, width), lambda i: (i, 0))
    lane = pl.BlockSpec((TQ, 128), lambda i: (i, 0))
    return pl.pallas_call(
        first_kernel,
        out_shape=(
            jax.ShapeDtypeStruct((rows, width), jnp.float32),
            jax.ShapeDtypeStruct((rows, 128), jnp.float32),
            jax.ShapeDtypeStruct((rows, 128), jnp.float32),
        ),
        grid=(rows // TQ,),
        in_specs=[rowblock, whole(keys), whole(values)],
        out_specs=(rowblock, lane, lane),
        compiler_params=pltpu.CompilerParams(vmem_limit_bytes=60 * 1024 * 1024),
        cost_estimate=pl.CostEstimate(
            flops=4 * rows * nk * width, transcendentals=rows * nk * H,
            bytes_accessed=2 * width * (rows + 2 * nk) + 4 * rows * width),
    )(queries, keys, values)


def attend_last(queries, lo, up, co, mlo, mup, acc, high, total, gain):
    rows, width = queries.shape
    nk = 2 * lo.shape[1] + co.shape[1]
    rowblock = pl.BlockSpec((TQ, width), lambda i: (i, 0))
    lane = pl.BlockSpec((TQ, 128), lambda i: (i, 0))
    return pl.pallas_call(
        last_kernel,
        out_shape=jax.ShapeDtypeStruct((rows, width), jnp.bfloat16),
        grid=(rows // TQ,),
        in_specs=[rowblock, whole(lo), whole(up), whole(co), whole(mlo), whole(mup),
                  rowblock, lane, lane, whole(gain)],
        out_specs=rowblock,
        scratch_shapes=[pltpu.VMEM((TQ, nk), jnp.float32),
                        pltpu.VMEM((TQ, width), jnp.float32)],
        compiler_params=pltpu.CompilerParams(vmem_limit_bytes=60 * 1024 * 1024),
    )(queries, lo, up, co, mlo, mup, acc, high, total, gain)


def on_device(queries, keys, values, out_gain, out_weight, adjacency, send_counts, coarse_index):
    bands = 16
    place = lax.axis_index(BAND)
    width = adjacency.shape[2]
    lower_rows = adjacency[0, 0]
    upper_rows = adjacency[0, 1]
    to_lower = jnp.stack([keys[lower_rows], values[lower_rows]], axis=0)
    to_upper = jnp.stack([keys[upper_rows], values[upper_rows]], axis=0)
    coarse = jnp.stack([keys[coarse_index], values[coarse_index]], axis=0)
    from_lower = shifted_2(to_upper, BAND, 1)
    from_upper = shifted_2(to_lower, BAND, -1)
    halves = lax.all_gather(coarse, "zhi", axis=1, tiled=True)
    everything = lax.all_gather(halves, ("y", "core"), axis=1, tiled=True)
    lower_peer = jnp.maximum(place - 1, 0)
    upper_peer = jnp.minimum(place + 1, bands - 1)
    slots = jnp.arange(width, dtype=jnp.int32)
    lower_live = (slots < send_counts[lower_peer, 1]) & (place > 0)
    upper_live = (slots < send_counts[upper_peer, 0]) & (place < bands - 1)
    mlo = lower_live.astype(jnp.float32)[None, :]
    mup = upper_live.astype(jnp.float32)[None, :]
    acc, high, total = attend_first(queries, keys, values)
    normed = attend_last(queries, from_lower, from_upper, everything, mlo, mup,
                         acc, high, total, out_gain[None, :])
    return jnp.dot(normed, out_weight, preferred_element_type=jnp.float32).astype(jnp.bfloat16)


def solution(mesh):
    grid = mesh.devices.reshape(mesh.devices.shape[0], 2, 4, 2)
    fine = jax.sharding.Mesh(grid, ("slide",) + BAND)
    rows = ("slide",) + BAND
    in_specs = (
        P(rows, None),
        P(rows, None),
        P(rows, None),
        P(),
        P(),
        P(rows, None, None),
        P("slide", None),
        P(rows),
    )
    out_specs = P(rows, None)
    return jax.shard_map(
        on_device, mesh=fine, in_specs=in_specs, out_specs=out_specs, check_vma=False
    )
```

```python
import functools
import jax
import jax.numpy as jnp
from jax import lax
from jax.experimental import pallas as pl
from jax.experimental.pallas import tpu as pltpu
from jax.sharding import PartitionSpec as P

H = 12
HD = 128
BAND = ("zhi", "y", "core")
TQ = 128


def shifted_2(block, axis, distance):
    devices = range(16)
    route = [(i - distance, i) for i in devices if i - distance in devices]
    return lax.ppermute(block, axis, route)


def scores(qh, kr, cols, mr):
    s = lax.dot_general(
        qh, kr[:, cols], (((1,), (1,)), ((), ())),
        preferred_element_type=jnp.float32,
    ) * (1.0 / HD**0.5)
    if mr is not None:
        s = jnp.where(mr[...] > 0.5, s, -1e30)
    return s


def first_kernel(q_ref, k_ref, v_ref, acc_ref, m_ref, l_ref):
    for h in range(H):
        cols = slice(h * HD, (h + 1) * HD)
        sc = scores(q_ref[:, cols], k_ref, cols, None)
        high = jnp.max(sc, axis=1, keepdims=True)
        w = jnp.exp(sc - high)
        acc_ref[:, cols] = jnp.dot(w.astype(jnp.bfloat16), v_ref[:, cols],
                                   preferred_element_type=jnp.float32)
        m_ref[:, h:h + 1] = high
        l_ref[:, h:h + 1] = jnp.sum(w, axis=1, keepdims=True)


def last_kernel(q_ref, lo_ref, up_ref, co_ref, mlo_ref, mup_ref, acc_ref, m_ref, l_ref,
                gain_ref, o_ref, s_ref, att_ref):
    n_b = lo_ref.shape[1]
    segs = [
        (lo_ref.at[0], lo_ref.at[1], 0, mlo_ref),
        (up_ref.at[0], up_ref.at[1], n_b, mup_ref),
        (co_ref.at[0], co_ref.at[1], 2 * n_b, None),
    ]
    for h in range(H):
        cols = slice(h * HD, (h + 1) * HD)
        qh = q_ref[:, cols]
        for kr, _, off, mr in segs:
            s_ref[:, off:off + kr.shape[0]] = scores(qh, kr, cols, mr)
        sc = s_ref[...]
        high_old = m_ref[:, h:h + 1]
        high = jnp.maximum(high_old, jnp.max(sc, axis=1, keepdims=True))
        factor = jnp.exp(high_old - high)
        w = jnp.exp(sc - high)
        total = l_ref[:, h:h + 1] * factor + jnp.sum(w, axis=1, keepdims=True)
        wb = w.astype(jnp.bfloat16)
        acc = acc_ref[:, cols] * factor
        for kr, vr, off, _ in segs:
            n = kr.shape[0]
            acc = acc + jnp.dot(wb[:, off:off + n], vr[:, cols],
                                preferred_element_type=jnp.float32)
        att_ref[:, cols] = acc / total
    att = att_ref[...]
    center = jnp.mean(att, axis=1, keepdims=True)
    shifted = att - center
    spread = jnp.mean(shifted * shifted, axis=1, keepdims=True)
    o_ref[...] = (shifted / jnp.sqrt(spread + 1e-05) * gain_ref[...]).astype(o_ref.dtype)


def whole(a):
    return pl.BlockSpec(a.shape, lambda i: (0,) * a.ndim)


def attend_first(queries, keys, values):
    rows, width = queries.shape
    nk = keys.shape[0]
    rowblock = pl.BlockSpec((TQ, width), lambda i: (i, 0))
    lane = pl.BlockSpec((TQ, 128), lambda i: (i, 0))
    return pl.pallas_call(
        first_kernel,
        out_shape=(
            jax.ShapeDtypeStruct((rows, width), jnp.float32),
            jax.ShapeDtypeStruct((rows, 128), jnp.float32),
            jax.ShapeDtypeStruct((rows, 128), jnp.float32),
        ),
        grid=(rows // TQ,),
        in_specs=[rowblock, whole(keys), whole(values)],
        out_specs=(rowblock, lane, lane),
        compiler_params=pltpu.CompilerParams(vmem_limit_bytes=60 * 1024 * 1024),
        cost_estimate=pl.CostEstimate(
            flops=4 * rows * nk * width, transcendentals=rows * nk * H,
            bytes_accessed=2 * width * (rows + 2 * nk) + 4 * rows * width),
    )(queries, keys, values)


def attend_last(queries, lo, up, co, mlo, mup, acc, high, total, gain):
    rows, width = queries.shape
    nk = 2 * lo.shape[1] + co.shape[1]
    rowblock = pl.BlockSpec((TQ, width), lambda i: (i, 0))
    lane = pl.BlockSpec((TQ, 128), lambda i: (i, 0))
    return pl.pallas_call(
        last_kernel,
        out_shape=jax.ShapeDtypeStruct((rows, width), jnp.bfloat16),
        grid=(rows // TQ,),
        in_specs=[rowblock, whole(lo), whole(up), whole(co), whole(mlo), whole(mup),
                  rowblock, lane, lane, whole(gain)],
        out_specs=rowblock,
        scratch_shapes=[pltpu.VMEM((TQ, nk), jnp.float32),
                        pltpu.VMEM((TQ, width), jnp.float32)],
        compiler_params=pltpu.CompilerParams(vmem_limit_bytes=60 * 1024 * 1024),
    )(queries, lo, up, co, mlo, mup, acc, high, total, gain)


def on_device(queries, keys, values, out_gain, out_weight, adjacency, send_counts, coarse_index):
    bands = 16
    place = lax.axis_index(BAND)
    width = adjacency.shape[2]
    lower_rows = adjacency[0, 0]
    upper_rows = adjacency[0, 1]
    to_lower = jnp.stack([keys[lower_rows], values[lower_rows]], axis=0)
    to_upper = jnp.stack([keys[upper_rows], values[upper_rows]], axis=0)
    coarse = jnp.stack([keys[coarse_index], values[coarse_index]], axis=0)
    from_lower = shifted_2(to_upper, BAND, 1)
    from_upper = shifted_2(to_lower, BAND, -1)
    partner = lax.ppermute(coarse, "zhi", [(0, 1), (1, 0)])
    halves = jnp.concatenate([coarse, partner], axis=1)
    everything = lax.all_gather(halves, ("y", "core"), axis=1, tiled=True)
    lower_peer = jnp.maximum(place - 1, 0)
    upper_peer = jnp.minimum(place + 1, bands - 1)
    slots = jnp.arange(width, dtype=jnp.int32)
    lower_live = (slots < send_counts[lower_peer, 1]) & (place > 0)
    upper_live = (slots < send_counts[upper_peer, 0]) & (place < bands - 1)
    mlo = lower_live.astype(jnp.float32)[None, :]
    mup = upper_live.astype(jnp.float32)[None, :]
    acc, high, total = attend_first(queries, keys, values)
    normed = attend_last(queries, from_lower, from_upper, everything, mlo, mup,
                         acc, high, total, out_gain[None, :])
    return jnp.dot(normed, out_weight, preferred_element_type=jnp.float32).astype(jnp.bfloat16)


def solution(mesh):
    grid = mesh.devices.reshape(mesh.devices.shape[0], 2, 4, 2)
    fine = jax.sharding.Mesh(grid, ("slide",) + BAND)
    rows = ("slide",) + BAND
    in_specs = (
        P(rows, None),
        P(rows, None),
        P(rows, None),
        P(),
        P(),
        P(rows, None, None),
        P("slide", None),
        P(rows),
    )
    out_specs = P(rows, None)
    return jax.shard_map(
        on_device, mesh=fine, in_specs=in_specs, out_specs=out_specs, check_vma=False
    )
```

```python
import functools
import jax
import jax.numpy as jnp
from jax import lax
from jax.experimental import pallas as pl
from jax.experimental.pallas import tpu as pltpu
from jax.sharding import PartitionSpec as P

H = 12
HD = 128
BAND = ("zhi", "y", "core")
TQ = 128


def shifted_2(block, axis, distance):
    devices = range(16)
    route = [(i - distance, i) for i in devices if i - distance in devices]
    return lax.ppermute(block, axis, route)


def attend_kernel(q_ref, k_ref, v_ref, lo_ref, up_ref, co_ref, mlo_ref, mup_ref,
                  gain_ref, w_ref, o_ref, s_ref, att_ref):
    h = pl.program_id(0)
    n_loc = k_ref.shape[0]
    n_b = lo_ref.shape[1]
    segs = [
        (k_ref, v_ref, 0, None),
        (lo_ref.at[0], lo_ref.at[1], n_loc, mlo_ref),
        (up_ref.at[0], up_ref.at[1], n_loc + n_b, mup_ref),
        (co_ref.at[0], co_ref.at[1], n_loc + 2 * n_b, None),
    ]
    scale = 1.0 / HD**0.5
    qh = q_ref[...]
    for kr, _, off, mr in segs:
        n = kr.shape[0]
        s = lax.dot_general(
            qh, kr[...], (((1,), (1,)), ((), ())),
            preferred_element_type=jnp.float32,
        ) * scale
        if mr is not None:
            s = jnp.where(mr[...] > 0.5, s, -1e30)
        s_ref[:, off:off + n] = s
    sc = s_ref[...]
    high = jnp.max(sc, axis=1, keepdims=True)
    w = jnp.exp(sc - high)
    total = jnp.sum(w, axis=1, keepdims=True)
    wb = w.astype(jnp.bfloat16)
    acc = None
    for kr, vr, off, _ in segs:
        n = kr.shape[0]
        part = jnp.dot(wb[:, off:off + n], vr[...],
                       preferred_element_type=jnp.float32)
        acc = part if acc is None else acc + part
    att_ref[h] = acc / total

    @pl.when(h == H - 1)
    def _():
        att = jnp.concatenate([att_ref[i] for i in range(H)], axis=1)
        center = jnp.mean(att, axis=1, keepdims=True)
        shifted = att - center
        spread = jnp.mean(shifted * shifted, axis=1, keepdims=True)
        normed = (shifted / jnp.sqrt(spread + 1e-05) * gain_ref[...]).astype(jnp.bfloat16)
        o_ref[...] = jnp.dot(normed, w_ref[...],
                             preferred_element_type=jnp.float32).astype(o_ref.dtype)


def attend(queries, keys, values, lo, up, co, mlo, mup, gain, weight):
    rows, width = queries.shape
    nk = keys.shape[0] + 2 * lo.shape[1] + co.shape[1]
    full2 = lambda a: pl.BlockSpec(a.shape, lambda h: (0,) * a.ndim)
    head2 = lambda a: pl.BlockSpec((a.shape[0], HD), lambda h: (0, h))
    head3 = lambda a: pl.BlockSpec((a.shape[0], a.shape[1], HD), lambda h: (0, 0, h))
    return pl.pallas_call(
        attend_kernel,
        out_shape=jax.ShapeDtypeStruct((rows, width), jnp.bfloat16),
        grid=(H,),
        in_specs=[
            head2(queries), head2(keys), head2(values), head3(lo), head3(up), head3(co),
            full2(mlo), full2(mup), full2(gain), full2(weight),
        ],
        out_specs=full2(queries),
        scratch_shapes=[
            pltpu.VMEM((rows, nk), jnp.float32),
            pltpu.VMEM((H, rows, HD), jnp.float32),
        ],
        compiler_params=pltpu.CompilerParams(vmem_limit_bytes=60 * 1024 * 1024),
    )(queries, keys, values, lo, up, co, mlo, mup, gain, weight)


def on_device(queries, keys, values, out_gain, out_weight, adjacency, send_counts, coarse_index):
    bands = 16
    place = lax.axis_index(BAND)
    width = adjacency.shape[2]
    lower_rows = adjacency[0, 0]
    upper_rows = adjacency[0, 1]
    to_lower = jnp.stack([keys[lower_rows], values[lower_rows]], axis=0)
    to_upper = jnp.stack([keys[upper_rows], values[upper_rows]], axis=0)
    coarse = jnp.stack([keys[coarse_index], values[coarse_index]], axis=0)
    from_lower = shifted_2(to_upper, BAND, 1)
    from_upper = shifted_2(to_lower, BAND, -1)
    halves = lax.all_gather(coarse, "zhi", axis=1, tiled=True)
    everything = lax.all_gather(halves, ("y", "core"), axis=1, tiled=True)
    lower_peer = jnp.maximum(place - 1, 0)
    upper_peer = jnp.minimum(place + 1, bands - 1)
    slots = jnp.arange(width, dtype=jnp.int32)
    lower_live = (slots < send_counts[lower_peer, 1]) & (place > 0)
    upper_live = (slots < send_counts[upper_peer, 0]) & (place < bands - 1)
    mlo = lower_live.astype(jnp.float32)[None, :]
    mup = upper_live.astype(jnp.float32)[None, :]
    return attend(queries, keys, values, from_lower, from_upper, everything,
                  mlo, mup, out_gain[None, :], out_weight)


def solution(mesh):
    grid = mesh.devices.reshape(mesh.devices.shape[0], 2, 4, 2)
    fine = jax.sharding.Mesh(grid, ("slide",) + BAND)
    rows = ("slide",) + BAND
    in_specs = (
        P(rows, None),
        P(rows, None),
        P(rows, None),
        P(),
        P(),
        P(rows, None, None),
        P("slide", None),
        P(rows),
    )
    out_specs = P(rows, None)
    return jax.shard_map(
        on_device, mesh=fine, in_specs=in_specs, out_specs=out_specs, check_vma=False
    )
```

```python
import functools
import jax
import jax.numpy as jnp
from jax import lax
from jax.experimental import pallas as pl
from jax.experimental.pallas import tpu as pltpu
from jax.sharding import PartitionSpec as P

H = 12
HD = 128
BAND = ("zhi", "y", "core")
TQ = 128


def shifted_2(block, axis, distance):
    devices = range(16)
    route = [(i - distance, i) for i in devices if i - distance in devices]
    return lax.ppermute(block, axis, route)


def attend_kernel(q_ref, k_ref, v_ref, lo_ref, up_ref, co_ref, mlo_ref, mup_ref,
                  gain_ref, w_ref, o_ref, s_ref, att_ref):
    n_loc = k_ref.shape[0]
    n_b = lo_ref.shape[1]
    n_c = co_ref.shape[1]
    segs = [
        (k_ref, v_ref, 0, None),
        (lo_ref.at[0], lo_ref.at[1], n_loc, mlo_ref),
        (up_ref.at[0], up_ref.at[1], n_loc + n_b, mup_ref),
        (co_ref.at[0], co_ref.at[1], n_loc + 2 * n_b, None),
    ]
    scale = 1.0 / HD**0.5
    for h in range(H):
        cols = slice(h * HD, (h + 1) * HD)
        qh = q_ref[:, cols]
        for kr, _, off, mr in segs:
            n = kr.shape[0]
            s = lax.dot_general(
                qh, kr[:, cols], (((1,), (1,)), ((), ())),
                preferred_element_type=jnp.float32,
            ) * scale
            if mr is not None:
                s = jnp.where(mr[...] > 0.5, s, -1e30)
            s_ref[:, off:off + n] = s
        sc = s_ref[...]
        high = jnp.max(sc, axis=1, keepdims=True)
        wb = jnp.exp((sc - high).astype(jnp.bfloat16))
        ones = jnp.ones((wb.shape[1], HD), jnp.bfloat16)
        total = jnp.dot(wb, ones, preferred_element_type=jnp.float32)
        acc = None
        for kr, vr, off, _ in segs:
            n = kr.shape[0]
            part = jnp.dot(wb[:, off:off + n], vr[:, cols],
                           preferred_element_type=jnp.float32)
            acc = part if acc is None else acc + part
        att_ref[:, cols] = acc / total
    att = att_ref[...]
    center = jnp.mean(att, axis=1, keepdims=True)
    shifted = att - center
    spread = jnp.mean(shifted * shifted, axis=1, keepdims=True)
    normed = (shifted / jnp.sqrt(spread + 1e-05) * gain_ref[...]).astype(jnp.bfloat16)
    o_ref[...] = jnp.dot(normed, w_ref[...],
                         preferred_element_type=jnp.float32).astype(o_ref.dtype)


def attend(queries, keys, values, lo, up, co, mlo, mup, gain, weight):
    rows, width = queries.shape
    nk = keys.shape[0] + 2 * lo.shape[1] + co.shape[1]
    full2 = lambda a: pl.BlockSpec(a.shape, lambda i: (0,) * a.ndim)
    return pl.pallas_call(
        attend_kernel,
        out_shape=jax.ShapeDtypeStruct((rows, width), jnp.bfloat16),
        grid=(rows // TQ,),
        in_specs=[
            pl.BlockSpec((TQ, width), lambda i: (i, 0)),
            full2(keys), full2(values), full2(lo), full2(up), full2(co),
            full2(mlo), full2(mup), full2(gain), full2(weight),
        ],
        out_specs=pl.BlockSpec((TQ, width), lambda i: (i, 0)),
        scratch_shapes=[
            pltpu.VMEM((TQ, nk), jnp.float32),
            pltpu.VMEM((TQ, width), jnp.float32),
        ],
        compiler_params=pltpu.CompilerParams(vmem_limit_bytes=60 * 1024 * 1024),
    )(queries, keys, values, lo, up, co, mlo, mup, gain, weight)


def on_device(queries, keys, values, out_gain, out_weight, adjacency, send_counts, coarse_index):
    bands = 16
    place = lax.axis_index(BAND)
    width = adjacency.shape[2]
    lower_rows = adjacency[0, 0]
    upper_rows = adjacency[0, 1]
    to_lower = jnp.stack([keys[lower_rows], values[lower_rows]], axis=0)
    to_upper = jnp.stack([keys[upper_rows], values[upper_rows]], axis=0)
    coarse = jnp.stack([keys[coarse_index], values[coarse_index]], axis=0)
    from_lower = shifted_2(to_upper, BAND, 1)
    from_upper = shifted_2(to_lower, BAND, -1)
    halves = lax.all_gather(coarse, "zhi", axis=1, tiled=True)
    everything = lax.all_gather(halves, ("y", "core"), axis=1, tiled=True)
    lower_peer = jnp.maximum(place - 1, 0)
    upper_peer = jnp.minimum(place + 1, bands - 1)
    slots = jnp.arange(width, dtype=jnp.int32)
    lower_live = (slots < send_counts[lower_peer, 1]) & (place > 0)
    upper_live = (slots < send_counts[upper_peer, 0]) & (place < bands - 1)
    mlo = lower_live.astype(jnp.float32)[None, :]
    mup = upper_live.astype(jnp.float32)[None, :]
    return attend(queries, keys, values, from_lower, from_upper, everything,
                  mlo, mup, out_gain[None, :], out_weight)


def solution(mesh):
    grid = mesh.devices.reshape(mesh.devices.shape[0], 2, 4, 2)
    fine = jax.sharding.Mesh(grid, ("slide",) + BAND)
    rows = ("slide",) + BAND
    in_specs = (
        P(rows, None),
        P(rows, None),
        P(rows, None),
        P(),
        P(),
        P(rows, None, None),
        P("slide", None),
        P(rows),
    )
    out_specs = P(rows, None)
    return jax.shard_map(
        on_device, mesh=fine, in_specs=in_specs, out_specs=out_specs, check_vma=False
    )
```

```python
import functools
import jax
import jax.numpy as jnp
from jax import lax
from jax.experimental import pallas as pl
from jax.experimental.pallas import tpu as pltpu
from jax.sharding import PartitionSpec as P

H = 12
HD = 128
BAND = ("zhi", "y", "core")
TQ = 128


def shifted_2(block, axis, distance):
    devices = range(16)
    route = [(i - distance, i) for i in devices if i - distance in devices]
    return lax.ppermute(block, axis, route)


def attend_kernel(q_ref, k_ref, v_ref, lo_ref, up_ref, co_ref, klo_ref, kup_ref, kco_ref,
                  mlo_ref, mup_ref, gain_ref, w_ref, o_ref, s_ref, att_ref):
    n_loc = k_ref.shape[1]
    n_b = lo_ref.shape[1]
    segs = [
        (k_ref, v_ref, 0, None),
        (klo_ref, lo_ref.at[1], n_loc, mlo_ref),
        (kup_ref, up_ref.at[1], n_loc + n_b, mup_ref),
        (kco_ref, co_ref.at[1], n_loc + 2 * n_b, None),
    ]
    scale = 1.0 / HD**0.5
    for h in range(H):
        cols = slice(h * HD, (h + 1) * HD)
        qh = q_ref[:, cols]
        for kr, _, off, mr in segs:
            n = kr.shape[1]
            s = jnp.dot(qh, kr[cols, :], preferred_element_type=jnp.float32) * scale
            if mr is not None:
                s = jnp.where(mr[...] > 0.5, s, -1e30)
            s_ref[:, off:off + n] = s
        sc = s_ref[...]
        high = jnp.max(sc, axis=1, keepdims=True)
        w = jnp.exp(sc - high)
        total = jnp.sum(w, axis=1, keepdims=True)
        wb = w.astype(jnp.bfloat16)
        acc = None
        for kr, vr, off, _ in segs:
            n = kr.shape[1]
            part = jnp.dot(wb[:, off:off + n], vr[:, cols],
                           preferred_element_type=jnp.float32)
            acc = part if acc is None else acc + part
        att_ref[:, cols] = acc / total
    att = att_ref[...]
    center = jnp.mean(att, axis=1, keepdims=True)
    shifted = att - center
    spread = jnp.mean(shifted * shifted, axis=1, keepdims=True)
    normed = (shifted / jnp.sqrt(spread + 1e-05) * gain_ref[...]).astype(jnp.bfloat16)
    o_ref[...] = jnp.dot(normed, w_ref[...],
                         preferred_element_type=jnp.float32).astype(o_ref.dtype)


def attend(queries, keys, values, lo, up, co, mlo, mup, gain, weight):
    rows, width = queries.shape
    nk = keys.shape[0] + 2 * lo.shape[1] + co.shape[1]
    keys = keys.T
    klo = lo[0].T
    kup = up[0].T
    kco = co[0].T
    full2 = lambda a: pl.BlockSpec(a.shape, lambda i: (0,) * a.ndim)
    return pl.pallas_call(
        attend_kernel,
        out_shape=jax.ShapeDtypeStruct((rows, width), jnp.bfloat16),
        grid=(rows // TQ,),
        in_specs=[
            pl.BlockSpec((TQ, width), lambda i: (i, 0)),
            full2(keys), full2(values), full2(lo), full2(up), full2(co),
            full2(klo), full2(kup), full2(kco), full2(mlo), full2(mup), full2(gain), full2(weight),
        ],
        out_specs=pl.BlockSpec((TQ, width), lambda i: (i, 0)),
        scratch_shapes=[
            pltpu.VMEM((TQ, nk), jnp.float32),
            pltpu.VMEM((TQ, width), jnp.float32),
        ],
        compiler_params=pltpu.CompilerParams(vmem_limit_bytes=60 * 1024 * 1024),
    )(queries, keys, values, lo, up, co, klo, kup, kco, mlo, mup, gain, weight)


def on_device(queries, keys, values, out_gain, out_weight, adjacency, send_counts, coarse_index):
    bands = 16
    place = lax.axis_index(BAND)
    width = adjacency.shape[2]
    lower_rows = adjacency[0, 0]
    upper_rows = adjacency[0, 1]
    to_lower = jnp.stack([keys[lower_rows], values[lower_rows]], axis=0)
    to_upper = jnp.stack([keys[upper_rows], values[upper_rows]], axis=0)
    coarse = jnp.stack([keys[coarse_index], values[coarse_index]], axis=0)
    from_lower = shifted_2(to_upper, BAND, 1)
    from_upper = shifted_2(to_lower, BAND, -1)
    halves = lax.all_gather(coarse, "zhi", axis=1, tiled=True)
    everything = lax.all_gather(halves, ("y", "core"), axis=1, tiled=True)
    lower_peer = jnp.maximum(place - 1, 0)
    upper_peer = jnp.minimum(place + 1, bands - 1)
    slots = jnp.arange(width, dtype=jnp.int32)
    lower_live = (slots < send_counts[lower_peer, 1]) & (place > 0)
    upper_live = (slots < send_counts[upper_peer, 0]) & (place < bands - 1)
    mlo = lower_live.astype(jnp.float32)[None, :]
    mup = upper_live.astype(jnp.float32)[None, :]
    return attend(queries, keys, values, from_lower, from_upper, everything,
                  mlo, mup, out_gain[None, :], out_weight)


def solution(mesh):
    grid = mesh.devices.reshape(mesh.devices.shape[0], 2, 4, 2)
    fine = jax.sharding.Mesh(grid, ("slide",) + BAND)
    rows = ("slide",) + BAND
    in_specs = (
        P(rows, None),
        P(rows, None),
        P(rows, None),
        P(),
        P(),
        P(rows, None, None),
        P("slide", None),
        P(rows),
    )
    out_specs = P(rows, None)
    return jax.shard_map(
        on_device, mesh=fine, in_specs=in_specs, out_specs=out_specs, check_vma=False
    )
```

```python
import functools
import jax
import jax.numpy as jnp
from jax import lax
from jax.experimental import pallas as pl
from jax.experimental.pallas import tpu as pltpu
from jax.sharding import PartitionSpec as P

H = 12
HD = 128
BAND = ("zhi", "y", "core")
TQ = 128


def shifted_2(block, axis, distance):
    devices = range(16)
    route = [(i - distance, i) for i in devices if i - distance in devices]
    return lax.ppermute(block, axis, route)


def attend_kernel(q_ref, k_ref, v_ref, lo_ref, up_ref, co_ref, mlo_ref, mup_ref,
                  gain_ref, o_ref, s_ref, att_ref):
    n_loc = k_ref.shape[0]
    n_b = lo_ref.shape[1]
    n_c = co_ref.shape[1]
    segs = [
        (k_ref, v_ref, 0, None),
        (lo_ref.at[0], lo_ref.at[1], n_loc, mlo_ref),
        (up_ref.at[0], up_ref.at[1], n_loc + n_b, mup_ref),
        (co_ref.at[0], co_ref.at[1], n_loc + 2 * n_b, None),
    ]
    scale = 1.0 / HD**0.5
    for h in range(H):
        cols = slice(h * HD, (h + 1) * HD)
        qh = q_ref[:, cols]
        for kr, _, off, mr in segs:
            n = kr.shape[0]
            s = lax.dot_general(
                qh, kr[:, cols], (((1,), (1,)), ((), ())),
                preferred_element_type=jnp.float32,
            ) * scale
            if mr is not None:
                s = jnp.where(mr[...] > 0.5, s, -1e30)
            s_ref[:, off:off + n] = s
        sc = s_ref[...]
        high = jnp.max(sc, axis=1, keepdims=True)
        w = jnp.exp(sc - high)
        total = jnp.sum(w, axis=1, keepdims=True)
        wb = w.astype(jnp.bfloat16)
        acc = None
        for kr, vr, off, _ in segs:
            n = kr.shape[0]
            part = jnp.dot(wb[:, off:off + n], vr[:, cols],
                           preferred_element_type=jnp.float32)
            acc = part if acc is None else acc + part
        att_ref[:, cols] = acc / total
    att = att_ref[...]
    center = jnp.mean(att, axis=1, keepdims=True)
    shifted = att - center
    spread = jnp.mean(shifted * shifted, axis=1, keepdims=True)
    o_ref[...] = (shifted / jnp.sqrt(spread + 1e-05) * gain_ref[...]).astype(o_ref.dtype)


def attend(queries, keys, values, lo, up, co, mlo, mup, gain):
    rows, width = queries.shape
    nk = keys.shape[0] + 2 * lo.shape[1] + co.shape[1]
    full2 = lambda a: pl.BlockSpec(a.shape, lambda i: (0,) * a.ndim)
    return pl.pallas_call(
        attend_kernel,
        out_shape=jax.ShapeDtypeStruct((rows, width), jnp.bfloat16),
        grid=(rows // TQ,),
        in_specs=[
            pl.BlockSpec((TQ, width), lambda i: (i, 0)),
            full2(keys), full2(values), full2(lo), full2(up), full2(co),
            full2(mlo), full2(mup), full2(gain),
        ],
        out_specs=pl.BlockSpec((TQ, width), lambda i: (i, 0)),
        scratch_shapes=[
            pltpu.VMEM((TQ, nk), jnp.float32),
            pltpu.VMEM((TQ, width), jnp.float32),
        ],
        compiler_params=pltpu.CompilerParams(vmem_limit_bytes=60 * 1024 * 1024),
    )(queries, keys, values, lo, up, co, mlo, mup, gain)


def on_device(queries, keys, values, out_gain, out_weight, adjacency, send_counts, coarse_index):
    bands = 16
    place = lax.axis_index(BAND)
    width = adjacency.shape[2]
    lower_rows = adjacency[0, 0]
    upper_rows = adjacency[0, 1]
    to_lower = jnp.stack([keys[lower_rows], values[lower_rows]], axis=0)
    to_upper = jnp.stack([keys[upper_rows], values[upper_rows]], axis=0)
    coarse = jnp.stack([keys[coarse_index], values[coarse_index]], axis=0)
    from_lower = shifted_2(to_upper, BAND, 1)
    from_upper = shifted_2(to_lower, BAND, -1)
    halves = lax.all_gather(coarse, "zhi", axis=1, tiled=True)
    everything = lax.all_gather(halves, ("y", "core"), axis=1, tiled=True)
    lower_peer = jnp.maximum(place - 1, 0)
    upper_peer = jnp.minimum(place + 1, bands - 1)
    slots = jnp.arange(width, dtype=jnp.int32)
    lower_live = (slots < send_counts[lower_peer, 1]) & (place > 0)
    upper_live = (slots < send_counts[upper_peer, 0]) & (place < bands - 1)
    mlo = lower_live.astype(jnp.float32)[None, :]
    mup = upper_live.astype(jnp.float32)[None, :]
    normed = attend(queries, keys, values, from_lower, from_upper, everything,
                    mlo, mup, out_gain[None, :])
    return jnp.dot(normed, out_weight, preferred_element_type=jnp.float32).astype(jnp.bfloat16)


def solution(mesh):
    grid = mesh.devices.reshape(mesh.devices.shape[0], 2, 4, 2)
    fine = jax.sharding.Mesh(grid, ("slide",) + BAND)
    rows = ("slide",) + BAND
    in_specs = (
        P(rows, None),
        P(rows, None),
        P(rows, None),
        P(),
        P(),
        P(rows, None, None),
        P("slide", None),
        P(rows),
    )
    out_specs = P(rows, None)
    return jax.shard_map(
        on_device, mesh=fine, in_specs=in_specs, out_specs=out_specs, check_vma=False
    )
```

```python
import functools
import jax
import jax.numpy as jnp
from jax import lax
from jax.experimental import pallas as pl
from jax.experimental.pallas import tpu as pltpu
from jax.sharding import PartitionSpec as P

H = 12
HD = 128
BAND = ("zhi", "y", "core")
TQ = 128


def shifted_2(block, axis, distance):
    devices = range(16)
    route = [(i - distance, i) for i in devices if i - distance in devices]
    return lax.ppermute(block, axis, route)


def attend_kernel(q_ref, k_ref, v_ref, lo_ref, up_ref, co_ref, mlo_ref, mup_ref,
                  gain_ref, w_hbm, o_ref, s_ref, att_ref, w_ref, w_sem):
    step = pl.program_id(0)
    w_copy = pltpu.make_async_copy(w_hbm, w_ref, w_sem.at[0])

    @pl.when(step == 0)
    def _():
        w_copy.start()

    n_loc = k_ref.shape[0]
    n_b = lo_ref.shape[1]
    n_c = co_ref.shape[1]
    segs = [
        (k_ref, v_ref, 0, None),
        (lo_ref.at[0], lo_ref.at[1], n_loc, mlo_ref),
        (up_ref.at[0], up_ref.at[1], n_loc + n_b, mup_ref),
        (co_ref.at[0], co_ref.at[1], n_loc + 2 * n_b, None),
    ]
    scale = 1.0 / HD**0.5
    for h in range(H):
        cols = slice(h * HD, (h + 1) * HD)
        qh = q_ref[:, cols]
        for kr, _, off, mr in segs:
            n = kr.shape[0]
            s = lax.dot_general(
                qh, kr[:, cols], (((1,), (1,)), ((), ())),
                preferred_element_type=jnp.float32,
            ) * scale
            if mr is not None:
                s = jnp.where(mr[...] > 0.5, s, -1e30)
            s_ref[:, off:off + n] = s
        sc = s_ref[...]
        high = jnp.max(sc, axis=1, keepdims=True)
        w = jnp.exp(sc - high)
        total = jnp.sum(w, axis=1, keepdims=True)
        wb = w.astype(jnp.bfloat16)
        acc = None
        for kr, vr, off, _ in segs:
            n = kr.shape[0]
            part = jnp.dot(wb[:, off:off + n], vr[:, cols],
                           preferred_element_type=jnp.float32)
            acc = part if acc is None else acc + part
        att_ref[:, cols] = acc / total
    att = att_ref[...]
    center = jnp.mean(att, axis=1, keepdims=True)
    shifted = att - center
    spread = jnp.mean(shifted * shifted, axis=1, keepdims=True)
    normed = (shifted / jnp.sqrt(spread + 1e-05) * gain_ref[...]).astype(jnp.bfloat16)

    @pl.when(step == 0)
    def _():
        w_copy.wait()

    o_ref[...] = jnp.dot(normed, w_ref[...],
                         preferred_element_type=jnp.float32).astype(o_ref.dtype)


def attend(queries, keys, values, lo, up, co, mlo, mup, gain, weight):
    rows, width = queries.shape
    nk = keys.shape[0] + 2 * lo.shape[1] + co.shape[1]
    full2 = lambda a: pl.BlockSpec(a.shape, lambda i: (0,) * a.ndim)
    return pl.pallas_call(
        attend_kernel,
        out_shape=jax.ShapeDtypeStruct((rows, width), jnp.bfloat16),
        grid=(rows // TQ,),
        in_specs=[
            pl.BlockSpec((TQ, width), lambda i: (i, 0)),
            full2(keys), full2(values), full2(lo), full2(up), full2(co),
            full2(mlo), full2(mup), full2(gain), pl.BlockSpec(memory_space=pl.ANY),
        ],
        out_specs=pl.BlockSpec((TQ, width), lambda i: (i, 0)),
        scratch_shapes=[
            pltpu.VMEM((TQ, nk), jnp.float32),
            pltpu.VMEM((TQ, width), jnp.float32),
            pltpu.VMEM(weight.shape, weight.dtype),
            pltpu.SemaphoreType.DMA((1,)),
        ],
        compiler_params=pltpu.CompilerParams(vmem_limit_bytes=60 * 1024 * 1024),
    )(queries, keys, values, lo, up, co, mlo, mup, gain, weight)


def on_device(queries, keys, values, out_gain, out_weight, adjacency, send_counts, coarse_index):
    bands = 16
    place = lax.axis_index(BAND)
    width = adjacency.shape[2]
    lower_rows = adjacency[0, 0]
    upper_rows = adjacency[0, 1]
    to_lower = jnp.stack([keys[lower_rows], values[lower_rows]], axis=0)
    to_upper = jnp.stack([keys[upper_rows], values[upper_rows]], axis=0)
    coarse = jnp.stack([keys[coarse_index], values[coarse_index]], axis=0)
    from_lower = shifted_2(to_upper, BAND, 1)
    from_upper = shifted_2(to_lower, BAND, -1)
    halves = lax.all_gather(coarse, "zhi", axis=1, tiled=True)
    everything = lax.all_gather(halves, ("y", "core"), axis=1, tiled=True)
    lower_peer = jnp.maximum(place - 1, 0)
    upper_peer = jnp.minimum(place + 1, bands - 1)
    slots = jnp.arange(width, dtype=jnp.int32)
    lower_live = (slots < send_counts[lower_peer, 1]) & (place > 0)
    upper_live = (slots < send_counts[upper_peer, 0]) & (place < bands - 1)
    mlo = lower_live.astype(jnp.float32)[None, :]
    mup = upper_live.astype(jnp.float32)[None, :]
    return attend(queries, keys, values, from_lower, from_upper, everything,
                  mlo, mup, out_gain[None, :], out_weight)


def solution(mesh):
    grid = mesh.devices.reshape(mesh.devices.shape[0], 2, 4, 2)
    fine = jax.sharding.Mesh(grid, ("slide",) + BAND)
    rows = ("slide",) + BAND
    in_specs = (
        P(rows, None),
        P(rows, None),
        P(rows, None),
        P(),
        P(),
        P(rows, None, None),
        P("slide", None),
        P(rows),
    )
    out_specs = P(rows, None)
    return jax.shard_map(
        on_device, mesh=fine, in_specs=in_specs, out_specs=out_specs, check_vma=False
    )
```

```python
import functools
import jax
import jax.numpy as jnp
from jax import lax
from jax.experimental import pallas as pl
from jax.experimental.pallas import tpu as pltpu
from jax.sharding import PartitionSpec as P

H = 12
HD = 128
BAND = ("zhi", "y", "core")
TQ = 128


def shifted_2(block, axis, distance):
    devices = range(16)
    route = [(i - distance, i) for i in devices if i - distance in devices]
    return lax.ppermute(block, axis, route)


def attend_kernel(q_ref, k_ref, v_ref, lo_ref, up_ref, co_ref, mlo_ref, mup_ref,
                  gain_ref, w_hbm, o_ref, s_ref, att_ref, w_ref, w_sem):
    step = pl.program_id(0)
    rows = pl.ds(pl.multiple_of(step * TQ, TQ), TQ)
    w_copy = pltpu.make_async_copy(w_hbm, w_ref, w_sem.at[0])

    @pl.when(step == 0)
    def _():
        w_copy.start()

    n_loc = k_ref.shape[0]
    n_b = lo_ref.shape[1]
    n_c = co_ref.shape[1]
    segs = [
        (k_ref, v_ref, 0, None),
        (lo_ref.at[0], lo_ref.at[1], n_loc, mlo_ref),
        (up_ref.at[0], up_ref.at[1], n_loc + n_b, mup_ref),
        (co_ref.at[0], co_ref.at[1], n_loc + 2 * n_b, None),
    ]
    scale = 1.0 / HD**0.5
    for h in range(H):
        cols = slice(h * HD, (h + 1) * HD)
        qh = q_ref[rows, cols]
        for kr, _, off, mr in segs:
            n = kr.shape[0]
            s = lax.dot_general(
                qh, kr[:, cols], (((1,), (1,)), ((), ())),
                preferred_element_type=jnp.float32,
            ) * scale
            if mr is not None:
                s = jnp.where(mr[...] > 0.5, s, -1e30)
            s_ref[:, off:off + n] = s
        sc = s_ref[...]
        high = jnp.max(sc, axis=1, keepdims=True)
        w = jnp.exp(sc - high)
        total = jnp.sum(w, axis=1, keepdims=True)
        wb = w.astype(jnp.bfloat16)
        acc = None
        for kr, vr, off, _ in segs:
            n = kr.shape[0]
            part = jnp.dot(wb[:, off:off + n], vr[:, cols],
                           preferred_element_type=jnp.float32)
            acc = part if acc is None else acc + part
        att_ref[:, cols] = acc / total
    att = att_ref[...]
    center = jnp.mean(att, axis=1, keepdims=True)
    shifted = att - center
    spread = jnp.mean(shifted * shifted, axis=1, keepdims=True)
    normed = (shifted / jnp.sqrt(spread + 1e-05) * gain_ref[...]).astype(jnp.bfloat16)

    @pl.when(step == 0)
    def _():
        w_copy.wait()

    o_ref[...] = jnp.dot(normed, w_ref[...],
                         preferred_element_type=jnp.float32).astype(o_ref.dtype)


def attend(queries, keys, values, lo, up, co, mlo, mup, gain, weight):
    rows, width = queries.shape
    nk = keys.shape[0] + 2 * lo.shape[1] + co.shape[1]
    full2 = lambda a: pl.BlockSpec(a.shape, lambda i: (0,) * a.ndim)
    return pl.pallas_call(
        attend_kernel,
        out_shape=jax.ShapeDtypeStruct((rows, width), jnp.bfloat16),
        grid=(rows // TQ,),
        in_specs=[
            pl.BlockSpec(memory_space=pltpu.VMEM),
            pl.BlockSpec(memory_space=pltpu.VMEM),
            pl.BlockSpec(memory_space=pltpu.VMEM), full2(lo), full2(up), full2(co),
            full2(mlo), full2(mup), full2(gain), pl.BlockSpec(memory_space=pl.ANY),
        ],
        out_specs=pl.BlockSpec((TQ, width), lambda i: (i, 0)),
        scratch_shapes=[
            pltpu.VMEM((TQ, nk), jnp.float32),
            pltpu.VMEM((TQ, width), jnp.float32),
            pltpu.VMEM(weight.shape, weight.dtype),
            pltpu.SemaphoreType.DMA((1,)),
        ],
        compiler_params=pltpu.CompilerParams(vmem_limit_bytes=40 * 1024 * 1024),
    )(queries, keys, values, lo, up, co, mlo, mup, gain, weight)


def on_device(queries, keys, values, out_gain, out_weight, adjacency, send_counts, coarse_index):
    bands = 16
    place = lax.axis_index(BAND)
    width = adjacency.shape[2]
    lower_rows = adjacency[0, 0]
    upper_rows = adjacency[0, 1]
    to_lower = jnp.stack([keys[lower_rows], values[lower_rows]], axis=0)
    to_upper = jnp.stack([keys[upper_rows], values[upper_rows]], axis=0)
    coarse = jnp.stack([keys[coarse_index], values[coarse_index]], axis=0)
    from_lower = shifted_2(to_upper, BAND, 1)
    from_upper = shifted_2(to_lower, BAND, -1)
    halves = lax.all_gather(coarse, "zhi", axis=1, tiled=True)
    everything = lax.all_gather(halves, ("y", "core"), axis=1, tiled=True)
    lower_peer = jnp.maximum(place - 1, 0)
    upper_peer = jnp.minimum(place + 1, bands - 1)
    slots = jnp.arange(width, dtype=jnp.int32)
    lower_live = (slots < send_counts[lower_peer, 1]) & (place > 0)
    upper_live = (slots < send_counts[upper_peer, 0]) & (place < bands - 1)
    mlo = lower_live.astype(jnp.float32)[None, :]
    mup = upper_live.astype(jnp.float32)[None, :]
    return attend(queries, keys, values, from_lower, from_upper, everything,
                  mlo, mup, out_gain[None, :], out_weight)


def solution(mesh):
    grid = mesh.devices.reshape(mesh.devices.shape[0], 2, 4, 2)
    fine = jax.sharding.Mesh(grid, ("slide",) + BAND)
    rows = ("slide",) + BAND
    in_specs = (
        P(rows, None),
        P(rows, None),
        P(rows, None),
        P(),
        P(),
        P(rows, None, None),
        P("slide", None),
        P(rows),
    )
    out_specs = P(rows, None)
    return jax.shard_map(
        on_device, mesh=fine, in_specs=in_specs, out_specs=out_specs, check_vma=False
    )
```

```python
import functools
import jax
import jax.numpy as jnp
from jax import lax
from jax.experimental import pallas as pl
from jax.experimental.pallas import tpu as pltpu
from jax.sharding import PartitionSpec as P

H = 12
HD = 128
BAND = ("zhi", "y", "core")
TQ = 128


def shifted_2(block, axis, distance):
    devices = range(16)
    route = [(i - distance, i) for i in devices if i - distance in devices]
    return lax.ppermute(block, axis, route)


def attend_kernel(q_ref, k_ref, v_ref, lo_ref, up_ref, co_ref, mlo_ref, mup_ref,
                  gain_ref, w_hbm, o_ref, s_ref, att_ref, w_ref, w_sem):
    step = pl.program_id(0)
    w_copy = pltpu.make_async_copy(w_hbm, w_ref, w_sem.at[0])

    @pl.when(step == 0)
    def _():
        w_copy.start()

    n_loc = k_ref.shape[0]
    n_b = lo_ref.shape[1]
    n_c = co_ref.shape[1]
    segs = [
        (k_ref, v_ref, 0, None),
        (lo_ref.at[0], lo_ref.at[1], n_loc, mlo_ref),
        (up_ref.at[0], up_ref.at[1], n_loc + n_b, mup_ref),
        (co_ref.at[0], co_ref.at[1], n_loc + 2 * n_b, None),
    ]
    scale = 1.0 / HD**0.5
    for h in range(H):
        cols = slice(h * HD, (h + 1) * HD)
        qh = q_ref[:, cols]
        for kr, _, off, mr in segs:
            n = kr.shape[0]
            s = lax.dot_general(
                qh, kr[:, cols], (((1,), (1,)), ((), ())),
                preferred_element_type=jnp.float32,
            ) * scale
            if mr is not None:
                s = jnp.where(mr[...] > 0.5, s, -1e30)
            s_ref[:, off:off + n] = s
        sc = s_ref[...]
        high = jnp.max(sc, axis=1, keepdims=True)
        w = jnp.exp(sc - high)
        total = jnp.sum(w, axis=1, keepdims=True)
        wb = w.astype(jnp.bfloat16)
        acc = None
        for kr, vr, off, _ in segs:
            n = kr.shape[0]
            part = jnp.dot(wb[:, off:off + n], vr[:, cols],
                           preferred_element_type=jnp.float32)
            acc = part if acc is None else acc + part
        att_ref[:, cols] = acc / total
    att = att_ref[...]
    center = jnp.mean(att, axis=1, keepdims=True)
    shifted = att - center
    spread = jnp.mean(shifted * shifted, axis=1, keepdims=True)
    normed = (shifted / jnp.sqrt(spread + 1e-05) * gain_ref[...]).astype(jnp.bfloat16)

    @pl.when(step == 0)
    def _():
        w_copy.wait()

    o_ref[...] = jnp.dot(normed, w_ref[...],
                         preferred_element_type=jnp.float32).astype(o_ref.dtype)


def attend(queries, keys, values, lo, up, co, mlo, mup, gain, weight):
    rows, width = queries.shape
    nk = keys.shape[0] + 2 * lo.shape[1] + co.shape[1]
    full2 = lambda a: pl.BlockSpec(a.shape, lambda i: (0,) * a.ndim)
    return pl.pallas_call(
        attend_kernel,
        out_shape=jax.ShapeDtypeStruct((rows, width), jnp.bfloat16),
        grid=(rows // TQ,),
        in_specs=[
            pl.BlockSpec((TQ, width), lambda i: (i, 0)),
            pl.BlockSpec(memory_space=pltpu.VMEM),
            pl.BlockSpec(memory_space=pltpu.VMEM),
            pl.BlockSpec(memory_space=pltpu.VMEM),
            pl.BlockSpec(memory_space=pltpu.VMEM), full2(co),
            full2(mlo), full2(mup), full2(gain), pl.BlockSpec(memory_space=pl.ANY),
        ],
        out_specs=pl.BlockSpec((TQ, width), lambda i: (i, 0)),
        scratch_shapes=[
            pltpu.VMEM((TQ, nk), jnp.float32),
            pltpu.VMEM((TQ, width), jnp.float32),
            pltpu.VMEM(weight.shape, weight.dtype),
            pltpu.SemaphoreType.DMA((1,)),
        ],
        compiler_params=pltpu.CompilerParams(vmem_limit_bytes=50 * 1024 * 1024),
    )(queries, keys, values, lo, up, co, mlo, mup, gain, weight)


def on_device(queries, keys, values, out_gain, out_weight, adjacency, send_counts, coarse_index):
    bands = 16
    place = lax.axis_index(BAND)
    width = adjacency.shape[2]
    lower_rows = adjacency[0, 0]
    upper_rows = adjacency[0, 1]
    to_lower = jnp.stack([keys[lower_rows], values[lower_rows]], axis=0)
    to_upper = jnp.stack([keys[upper_rows], values[upper_rows]], axis=0)
    coarse = jnp.stack([keys[coarse_index], values[coarse_index]], axis=0)
    from_lower = shifted_2(to_upper, BAND, 1)
    from_upper = shifted_2(to_lower, BAND, -1)
    halves = lax.all_gather(coarse, "zhi", axis=1, tiled=True)
    everything = lax.all_gather(halves, ("y", "core"), axis=1, tiled=True)
    lower_peer = jnp.maximum(place - 1, 0)
    upper_peer = jnp.minimum(place + 1, bands - 1)
    slots = jnp.arange(width, dtype=jnp.int32)
    lower_live = (slots < send_counts[lower_peer, 1]) & (place > 0)
    upper_live = (slots < send_counts[upper_peer, 0]) & (place < bands - 1)
    mlo = lower_live.astype(jnp.float32)[None, :]
    mup = upper_live.astype(jnp.float32)[None, :]
    return attend(queries, keys, values, from_lower, from_upper, everything,
                  mlo, mup, out_gain[None, :], out_weight)


def solution(mesh):
    grid = mesh.devices.reshape(mesh.devices.shape[0], 2, 4, 2)
    fine = jax.sharding.Mesh(grid, ("slide",) + BAND)
    rows = ("slide",) + BAND
    in_specs = (
        P(rows, None),
        P(rows, None),
        P(rows, None),
        P(),
        P(),
        P(rows, None, None),
        P("slide", None),
        P(rows),
    )
    out_specs = P(rows, None)
    return jax.shard_map(
        on_device, mesh=fine, in_specs=in_specs, out_specs=out_specs, check_vma=False
    )
```

```python
import functools
import jax
import jax.numpy as jnp
from jax import lax
from jax.experimental import pallas as pl
from jax.experimental.pallas import tpu as pltpu
from jax.sharding import PartitionSpec as P

H = 12
HD = 128
BAND = ("zhi", "y", "core")
TQ = 256


def shifted_2(block, axis, distance):
    devices = range(16)
    route = [(i - distance, i) for i in devices if i - distance in devices]
    return lax.ppermute(block, axis, route)


def attend_kernel(q_ref, k_ref, v_ref, lo_ref, up_ref, co_ref, mlo_ref, mup_ref,
                  gain_ref, w_hbm, o_ref, s_ref, att_ref, w_ref, w_sem):
    step = pl.program_id(0)
    w_copy = pltpu.make_async_copy(w_hbm, w_ref, w_sem.at[0])

    @pl.when(step == 0)
    def _():
        w_copy.start()

    n_loc = k_ref.shape[0]
    n_b = lo_ref.shape[1]
    n_c = co_ref.shape[1]
    segs = [
        (k_ref, v_ref, 0, None),
        (lo_ref.at[0], lo_ref.at[1], n_loc, mlo_ref),
        (up_ref.at[0], up_ref.at[1], n_loc + n_b, mup_ref),
        (co_ref.at[0], co_ref.at[1], n_loc + 2 * n_b, None),
    ]
    scale = 1.0 / HD**0.5
    for h in range(H):
        cols = slice(h * HD, (h + 1) * HD)
        qh = q_ref[:, cols]
        for kr, _, off, mr in segs:
            n = kr.shape[0]
            s = lax.dot_general(
                qh, kr[:, cols], (((1,), (1,)), ((), ())),
                preferred_element_type=jnp.float32,
            ) * scale
            if mr is not None:
                s = jnp.where(mr[...] > 0.5, s, -1e30)
            s_ref[:, off:off + n] = s
        sc = s_ref[...]
        high = jnp.max(sc, axis=1, keepdims=True)
        w = jnp.exp(sc - high)
        total = jnp.sum(w, axis=1, keepdims=True)
        wb = w.astype(jnp.bfloat16)
        acc = None
        for kr, vr, off, _ in segs:
            n = kr.shape[0]
            part = jnp.dot(wb[:, off:off + n], vr[:, cols],
                           preferred_element_type=jnp.float32)
            acc = part if acc is None else acc + part
        att_ref[:, cols] = acc / total
    att = att_ref[...]
    center = jnp.mean(att, axis=1, keepdims=True)
    shifted = att - center
    spread = jnp.mean(shifted * shifted, axis=1, keepdims=True)
    normed = (shifted / jnp.sqrt(spread + 1e-05) * gain_ref[...]).astype(jnp.bfloat16)

    @pl.when(step == 0)
    def _():
        w_copy.wait()

    o_ref[...] = jnp.dot(normed, w_ref[...],
                         preferred_element_type=jnp.float32).astype(o_ref.dtype)


def attend(queries, keys, values, lo, up, co, mlo, mup, gain, weight):
    rows, width = queries.shape
    nk = keys.shape[0] + 2 * lo.shape[1] + co.shape[1]
    full2 = lambda a: pl.BlockSpec(a.shape, lambda i: (0,) * a.ndim)
    return pl.pallas_call(
        attend_kernel,
        out_shape=jax.ShapeDtypeStruct((rows, width), jnp.bfloat16),
        grid=(rows // TQ,),
        in_specs=[
            pl.BlockSpec((TQ, width), lambda i: (i, 0)),
            full2(keys), full2(values), full2(lo), full2(up), full2(co),
            full2(mlo), full2(mup), full2(gain), pl.BlockSpec(memory_space=pl.ANY),
        ],
        out_specs=pl.BlockSpec((TQ, width), lambda i: (i, 0)),
        scratch_shapes=[
            pltpu.VMEM((TQ, nk), jnp.float32),
            pltpu.VMEM((TQ, width), jnp.float32),
            pltpu.VMEM(weight.shape, weight.dtype),
            pltpu.SemaphoreType.DMA((1,)),
        ],
        compiler_params=pltpu.CompilerParams(vmem_limit_bytes=60 * 1024 * 1024),
    )(queries, keys, values, lo, up, co, mlo, mup, gain, weight)


def on_device(queries, keys, values, out_gain, out_weight, adjacency, send_counts, coarse_index):
    bands = 16
    place = lax.axis_index(BAND)
    width = adjacency.shape[2]
    lower_rows = adjacency[0, 0]
    upper_rows = adjacency[0, 1]
    to_lower = jnp.stack([keys[lower_rows], values[lower_rows]], axis=0)
    to_upper = jnp.stack([keys[upper_rows], values[upper_rows]], axis=0)
    coarse = jnp.stack([keys[coarse_index], values[coarse_index]], axis=0)
    from_lower = shifted_2(to_upper, BAND, 1)
    from_upper = shifted_2(to_lower, BAND, -1)
    halves = lax.all_gather(coarse, "zhi", axis=1, tiled=True)
    everything = lax.all_gather(halves, ("y", "core"), axis=1, tiled=True)
    lower_peer = jnp.maximum(place - 1, 0)
    upper_peer = jnp.minimum(place + 1, bands - 1)
    slots = jnp.arange(width, dtype=jnp.int32)
    lower_live = (slots < send_counts[lower_peer, 1]) & (place > 0)
    upper_live = (slots < send_counts[upper_peer, 0]) & (place < bands - 1)
    mlo = lower_live.astype(jnp.float32)[None, :]
    mup = upper_live.astype(jnp.float32)[None, :]
    return attend(queries, keys, values, from_lower, from_upper, everything,
                  mlo, mup, out_gain[None, :], out_weight)


def solution(mesh):
    grid = mesh.devices.reshape(mesh.devices.shape[0], 2, 4, 2)
    fine = jax.sharding.Mesh(grid, ("slide",) + BAND)
    rows = ("slide",) + BAND
    in_specs = (
        P(rows, None),
        P(rows, None),
        P(rows, None),
        P(),
        P(),
        P(rows, None, None),
        P("slide", None),
        P(rows),
    )
    out_specs = P(rows, None)
    return jax.shard_map(
        on_device, mesh=fine, in_specs=in_specs, out_specs=out_specs, check_vma=False
    )
```

```python
import functools
import jax
import jax.numpy as jnp
from jax import lax
from jax.experimental import pallas as pl
from jax.experimental.pallas import tpu as pltpu
from jax.sharding import PartitionSpec as P

H = 12
HD = 128
BAND = ("zhi", "y", "core")
TQ = 512


def shifted_2(block, axis, distance):
    devices = range(16)
    route = [(i - distance, i) for i in devices if i - distance in devices]
    return lax.ppermute(block, axis, route)


def attend_kernel(q_ref, k_ref, v_ref, lo_ref, up_ref, co_ref, mlo_ref, mup_ref,
                  gain_ref, w_hbm, o_ref, s_ref, att_ref, w_ref, w_sem):
    step = pl.program_id(0)
    w_copy = pltpu.make_async_copy(w_hbm, w_ref, w_sem.at[0])

    @pl.when(step == 0)
    def _():
        w_copy.start()

    n_loc = k_ref.shape[0]
    n_b = lo_ref.shape[1]
    n_c = co_ref.shape[1]
    segs = [
        (k_ref, v_ref, 0, None),
        (lo_ref.at[0], lo_ref.at[1], n_loc, mlo_ref),
        (up_ref.at[0], up_ref.at[1], n_loc + n_b, mup_ref),
        (co_ref.at[0], co_ref.at[1], n_loc + 2 * n_b, None),
    ]
    scale = 1.0 / HD**0.5
    for h in range(H):
        cols = slice(h * HD, (h + 1) * HD)
        qh = q_ref[:, cols]
        for kr, _, off, mr in segs:
            n = kr.shape[0]
            s = lax.dot_general(
                qh, kr[:, cols], (((1,), (1,)), ((), ())),
                preferred_element_type=jnp.float32,
            ) * scale
            if mr is not None:
                s = jnp.where(mr[...] > 0.5, s, -1e30)
            s_ref[:, off:off + n] = s
        sc = s_ref[...]
        high = jnp.max(sc, axis=1, keepdims=True)
        w = jnp.exp(sc - high)
        total = jnp.sum(w, axis=1, keepdims=True)
        wb = w.astype(jnp.bfloat16)
        acc = None
        for kr, vr, off, _ in segs:
            n = kr.shape[0]
            part = jnp.dot(wb[:, off:off + n], vr[:, cols],
                           preferred_element_type=jnp.float32)
            acc = part if acc is None else acc + part
        att_ref[:, cols] = acc / total
    att = att_ref[...]
    center = jnp.mean(att, axis=1, keepdims=True)
    shifted = att - center
    spread = jnp.mean(shifted * shifted, axis=1, keepdims=True)
    normed = (shifted / jnp.sqrt(spread + 1e-05) * gain_ref[...]).astype(jnp.bfloat16)

    @pl.when(step == 0)
    def _():
        w_copy.wait()

    o_ref[...] = jnp.dot(normed, w_ref[...],
                         preferred_element_type=jnp.float32).astype(o_ref.dtype)


def attend(queries, keys, values, lo, up, co, mlo, mup, gain, weight):
    rows, width = queries.shape
    nk = keys.shape[0] + 2 * lo.shape[1] + co.shape[1]
    full2 = lambda a: pl.BlockSpec(a.shape, lambda i: (0,) * a.ndim)
    return pl.pallas_call(
        attend_kernel,
        out_shape=jax.ShapeDtypeStruct((rows, width), jnp.bfloat16),
        grid=(rows // TQ,),
        in_specs=[
            pl.BlockSpec((TQ, width), lambda i: (i, 0)),
            full2(keys), full2(values), full2(lo), full2(up), full2(co),
            full2(mlo), full2(mup), full2(gain), pl.BlockSpec(memory_space=pl.ANY),
        ],
        out_specs=pl.BlockSpec((TQ, width), lambda i: (i, 0)),
        scratch_shapes=[
            pltpu.VMEM((TQ, nk), jnp.float32),
            pltpu.VMEM((TQ, width), jnp.float32),
            pltpu.VMEM(weight.shape, weight.dtype),
            pltpu.SemaphoreType.DMA((1,)),
        ],
        compiler_params=pltpu.CompilerParams(vmem_limit_bytes=60 * 1024 * 1024),
    )(queries, keys, values, lo, up, co, mlo, mup, gain, weight)


def on_device(queries, keys, values, out_gain, out_weight, adjacency, send_counts, coarse_index):
    bands = 16
    place = lax.axis_index(BAND)
    width = adjacency.shape[2]
    lower_rows = adjacency[0, 0]
    upper_rows = adjacency[0, 1]
    to_lower = jnp.stack([keys[lower_rows], values[lower_rows]], axis=0)
    to_upper = jnp.stack([keys[upper_rows], values[upper_rows]], axis=0)
    coarse = jnp.stack([keys[coarse_index], values[coarse_index]], axis=0)
    from_lower = shifted_2(to_upper, BAND, 1)
    from_upper = shifted_2(to_lower, BAND, -1)
    halves = lax.all_gather(coarse, "zhi", axis=1, tiled=True)
    everything = lax.all_gather(halves, ("y", "core"), axis=1, tiled=True)
    lower_peer = jnp.maximum(place - 1, 0)
    upper_peer = jnp.minimum(place + 1, bands - 1)
    slots = jnp.arange(width, dtype=jnp.int32)
    lower_live = (slots < send_counts[lower_peer, 1]) & (place > 0)
    upper_live = (slots < send_counts[upper_peer, 0]) & (place < bands - 1)
    mlo = lower_live.astype(jnp.float32)[None, :]
    mup = upper_live.astype(jnp.float32)[None, :]
    return attend(queries, keys, values, from_lower, from_upper, everything,
                  mlo, mup, out_gain[None, :], out_weight)


def solution(mesh):
    grid = mesh.devices.reshape(mesh.devices.shape[0], 2, 4, 2)
    fine = jax.sharding.Mesh(grid, ("slide",) + BAND)
    rows = ("slide",) + BAND
    in_specs = (
        P(rows, None),
        P(rows, None),
        P(rows, None),
        P(),
        P(),
        P(rows, None, None),
        P("slide", None),
        P(rows),
    )
    out_specs = P(rows, None)
    return jax.shard_map(
        on_device, mesh=fine, in_specs=in_specs, out_specs=out_specs, check_vma=False
    )
```

```python
import functools
import jax
import jax.numpy as jnp
from jax import lax
from jax.experimental import pallas as pl
from jax.experimental.pallas import tpu as pltpu
from jax.sharding import PartitionSpec as P

H = 12
HD = 128
BAND = ("zhi", "y", "core")
TQ = 512


def shifted_2(block, axis, distance):
    devices = range(16)
    route = [(i - distance, i) for i in devices if i - distance in devices]
    return lax.ppermute(block, axis, route)


def attend_kernel(q_ref, k_ref, v_ref, lo_ref, up_ref, co_ref, mlo_ref, mup_ref,
                  gain_ref, w_hbm, o_ref, s_ref, att_ref, w_ref, w_sem):
    step = pl.program_id(0)
    w_copy = pltpu.make_async_copy(w_hbm, w_ref, w_sem.at[0])

    @pl.when(step == 0)
    def _():
        w_copy.start()

    n_loc = k_ref.shape[0]
    n_b = lo_ref.shape[1]
    n_c = co_ref.shape[1]
    segs = [
        (k_ref, v_ref, 0, None),
        (lo_ref.at[0], lo_ref.at[1], n_loc, mlo_ref),
        (up_ref.at[0], up_ref.at[1], n_loc + n_b, mup_ref),
        (co_ref.at[0], co_ref.at[1], n_loc + 2 * n_b, None),
    ]
    scale = 1.0 / HD**0.5
    for h in range(H):
        cols = slice(h * HD, (h + 1) * HD)
        qh = q_ref[:, cols]
        for kr, _, off, mr in segs:
            n = kr.shape[0]
            s = lax.dot_general(
                qh, kr[:, cols], (((1,), (1,)), ((), ())),
                preferred_element_type=jnp.float32,
            ) * scale
            if mr is not None:
                s = jnp.where(mr[...] > 0.5, s, -1e30)
            s_ref[:, off:off + n] = s
        sc = s_ref[...]
        high = jnp.max(sc, axis=1, keepdims=True)
        w = jnp.exp(sc - high)
        total = jnp.sum(w, axis=1, keepdims=True)
        wb = w.astype(jnp.bfloat16)
        acc = None
        for kr, vr, off, _ in segs:
            n = kr.shape[0]
            part = jnp.dot(wb[:, off:off + n], vr[:, cols],
                           preferred_element_type=jnp.float32)
            acc = part if acc is None else acc + part
        att_ref[:, cols] = acc / total
    att = att_ref[...]
    center = jnp.mean(att, axis=1, keepdims=True)
    shifted = att - center
    spread = jnp.mean(shifted * shifted, axis=1, keepdims=True)
    normed = (shifted / jnp.sqrt(spread + 1e-05) * gain_ref[...]).astype(jnp.bfloat16)

    @pl.when(step == 0)
    def _():
        w_copy.wait()

    o_ref[...] = jnp.dot(normed, w_ref[...],
                         preferred_element_type=jnp.float32).astype(o_ref.dtype)


def attend(queries, keys, values, lo, up, co, mlo, mup, gain, weight):
    rows, width = queries.shape
    nk = keys.shape[0] + 2 * lo.shape[1] + co.shape[1]
    full2 = lambda a: pl.BlockSpec(a.shape, lambda i: (0,) * a.ndim)
    return pl.pallas_call(
        attend_kernel,
        out_shape=jax.ShapeDtypeStruct((rows, width), jnp.bfloat16),
        grid=(rows // TQ,),
        in_specs=[
            pl.BlockSpec(memory_space=pltpu.VMEM),
            pl.BlockSpec(memory_space=pltpu.VMEM),
            pl.BlockSpec(memory_space=pltpu.VMEM), full2(lo), full2(up), full2(co),
            full2(mlo), full2(mup), full2(gain), pl.BlockSpec(memory_space=pl.ANY),
        ],
        out_specs=pl.BlockSpec((TQ, width), lambda i: (i, 0)),
        scratch_shapes=[
            pltpu.VMEM((TQ, nk), jnp.float32),
            pltpu.VMEM((TQ, width), jnp.float32),
            pltpu.VMEM(weight.shape, weight.dtype),
            pltpu.SemaphoreType.DMA((1,)),
        ],
        compiler_params=pltpu.CompilerParams(vmem_limit_bytes=50 * 1024 * 1024),
    )(queries, keys, values, lo, up, co, mlo, mup, gain, weight)


def on_device(queries, keys, values, out_gain, out_weight, adjacency, send_counts, coarse_index):
    bands = 16
    place = lax.axis_index(BAND)
    width = adjacency.shape[2]
    lower_rows = adjacency[0, 0]
    upper_rows = adjacency[0, 1]
    to_lower = jnp.stack([keys[lower_rows], values[lower_rows]], axis=0)
    to_upper = jnp.stack([keys[upper_rows], values[upper_rows]], axis=0)
    coarse = jnp.stack([keys[coarse_index], values[coarse_index]], axis=0)
    from_lower = shifted_2(to_upper, BAND, 1)
    from_upper = shifted_2(to_lower, BAND, -1)
    halves = lax.all_gather(coarse, "zhi", axis=1, tiled=True)
    everything = lax.all_gather(halves, ("y", "core"), axis=1, tiled=True)
    lower_peer = jnp.maximum(place - 1, 0)
    upper_peer = jnp.minimum(place + 1, bands - 1)
    slots = jnp.arange(width, dtype=jnp.int32)
    lower_live = (slots < send_counts[lower_peer, 1]) & (place > 0)
    upper_live = (slots < send_counts[upper_peer, 0]) & (place < bands - 1)
    mlo = lower_live.astype(jnp.float32)[None, :]
    mup = upper_live.astype(jnp.float32)[None, :]
    return attend(queries, keys, values, from_lower, from_upper, everything,
                  mlo, mup, out_gain[None, :], out_weight)


def solution(mesh):
    grid = mesh.devices.reshape(mesh.devices.shape[0], 2, 4, 2)
    fine = jax.sharding.Mesh(grid, ("slide",) + BAND)
    rows = ("slide",) + BAND
    in_specs = (
        P(rows, None),
        P(rows, None),
        P(rows, None),
        P(),
        P(),
        P(rows, None, None),
        P("slide", None),
        P(rows),
    )
    out_specs = P(rows, None)
    return jax.shard_map(
        on_device, mesh=fine, in_specs=in_specs, out_specs=out_specs, check_vma=False
    )
```
